512 devices in a mesh: dp: 64 (over x, z, core), cent: 8 (over y).
Axes of the slice: x: 4, y: 8, z: 8, core: 2. Of those that a mesh axis runs over, the one named last changes fastest.
Arguments:
- vectors: bfloat16 [65536, 768], P('dp'), may hold values from -64 to 64
- centroids: bfloat16 [8192, 768], P('cent'), may hold values from -5 to 5
- prior_mass: float32 [8192], P('cent'), may hold values from 0.5 to 8
- assign: int32 [65536], P('dp'), may hold values from 0 to 8191, as said below
- owner_of: int32 [8192], replicated, may hold values from 0 to 63, as said below
- rotation: bfloat16 [768, 768], replicated, may hold values from -0.21875 to 0.21875
Outputs:
- new_centroids: float32 [8, 1024, 768], P('cent', 'dp')
- moments: float32 [64, 16, 768], P('dp', None, 'cent')
The draws below stay inside these ranges and needn't reach their ends.
Inputs may be any that keep to these rules, and one draw needn't show every extreme that they name: `assign`: of the 1024 vectors of each dp index, exactly 128 have their list in each block of 1024 consecutive lists; of those, at most 8 have lists of one owner, and for each block of lists one owner, the same for every dp index, receives exactly 8 from every dp index. `owner_of`: each owner holds exactly 16 lists of each block of 1024 consecutive lists.
All inputs are finite; a program needn't handle non-finite values.
Results may differ from the reference program's by a relative error of at most 0.0033.
Values may be sent and summed in bfloat16 or wider, within the bound.
A program may use at most 64 MiB of HBM per device.

```python
import math
import jax
import jax.numpy as jnp
from jax import lax

D = 768
K = 8192
M = 48
TOK_DEV = 1024
N = 65536
KC = 1024
CAP = 8
N_DP = 64
N_CENT = 8


def centroid_table(key):
    base_key = jax.random.fold_in(key, 101)
    table = jnp.clip(jax.random.normal(base_key, (K, D), jnp.float32), -5.0, 5.0)
    return table.astype(jnp.bfloat16).astype(jnp.float32)


def draw_centroids(key, part):
    return centroid_table(key).astype(jnp.bfloat16)


def draw_vectors(key, part):
    key_list = jax.random.split(jax.random.fold_in(key, 202), 1)
    row_vals = jnp.clip(jax.random.normal(key_list[0], (N, D), jnp.float32), -6.0, 6.0)
    return row_vals.astype(jnp.bfloat16)


def routing_tables(key):
    base_key = jax.random.fold_in(key, 303)
    key_own, key_grade, key_full, key_pick, key_member, key_place = jax.random.split(base_key, 6)
    per_shard = TOK_DEV // N_CENT
    slot_total = N_DP * CAP
    perms = jax.vmap(lambda sub_key: jax.random.permutation(sub_key, KC))(jax.random.split(key_own, N_CENT)).astype(jnp.int32)
    owner_table = (perms % N_DP).reshape(K).astype(jnp.int32)
    inverse = jnp.argsort(perms, axis=1).astype(jnp.int32)
    quality_rank = jax.random.randint(key_grade, (N_CENT, N_DP), 0, 4)
    preferred_list = jax.random.randint(key_full, (N_CENT,), 0, N_DP)
    owner_span = jnp.arange(N_DP, dtype=jnp.int32)
    extra_reward = quality_rank * 256 + jnp.where(owner_span[None, :] == preferred_list[:, None], 2048, 0)
    slot_holder = jnp.arange(slot_total, dtype=jnp.int32) // CAP
    random_jitter = jax.random.randint(key_pick, (N_DP, N_CENT, slot_total), 0, 1024)
    merit_value = random_jitter + extra_reward[:, slot_holder][None, :, :]
    ranked = merit_value * 4096 + jnp.arange(slot_total, dtype=jnp.int32)[None, None, :]
    _, chosen = lax.top_k(ranked, per_shard)
    owner_ids = (chosen // CAP).astype(jnp.int32)
    member = jax.random.randint(key_member, (N_DP, N_CENT, per_shard), 0, KC // N_DP)
    shard_grid = jnp.broadcast_to(jnp.arange(N_CENT, dtype=jnp.int32)[None, :, None], owner_ids.shape)
    list_ids = shard_grid * KC + inverse[shard_grid, owner_ids + N_DP * member]
    flat_ids = list_ids.reshape(N_DP, TOK_DEV).astype(jnp.int32)
    orders = jax.vmap(lambda sub_key: jax.random.permutation(sub_key, TOK_DEV))(jax.random.split(key_place, N_DP))
    placed = jax.vmap(lambda spots, values: jnp.zeros((TOK_DEV,), jnp.int32).at[spots].set(values))(orders, flat_ids)
    return (owner_table, placed.reshape(N).astype(jnp.int32))


def draw_assign(key, part):
    return routing_tables(key)[1].astype(jnp.int32)


def draw_owner_of(key, part):
    return routing_tables(key)[0].astype(jnp.int32)


def shard_levels(rng, extent, shards, low, largest):
    loudness = 1.0
    for position, parts in shards:
        steps = jax.random.uniform(jax.random.fold_in(jax.random.fold_in(rng, 6), position), (parts,), jnp.float32, low / len(shards), largest / len(shards))
        loudness = loudness * jnp.repeat(jnp.exp(steps), extent[position] // parts).reshape((-1,) + (1,) * (len(extent) - 1 - position))
    return loudness


def gaussian(own_key, extent, width, bound, kind=jnp.bfloat16):
    result = width * jax.random.normal(own_key, extent, jnp.float32)
    return jnp.clip(result, min=-bound, max=bound).astype(kind)


def setup_inputs(seed: int = 0) -> dict:
    arg_keys = jax.random.split(jax.random.key(seed), 7)
    vectors = draw_vectors(jax.random.fold_in(arg_keys[6], 71), 0)
    centroids = draw_centroids(jax.random.fold_in(arg_keys[6], 71), 0)
    prior_mass = jnp.clip(jnp.exp(math.log(8.0) - 2.7725887 * jax.random.uniform(arg_keys[2], (K,), jnp.float32) ** shard_levels(arg_keys[2], (K,), ((0, 8),), -0.2, 0.2)), 0.5, 8.0)
    assign = draw_assign(jax.random.fold_in(arg_keys[6], 71), 0)
    owner_of = draw_owner_of(jax.random.fold_in(arg_keys[6], 71), 0)
    rotation = gaussian(arg_keys[5], (D, D), D ** -0.5, 0.21875)
    return dict(vectors=vectors, centroids=centroids, prior_mass=prior_mass, assign=assign, owner_of=owner_of, rotation=rotation)


def reference(vectors, centroids, prior_mass, assign, owner_of, rotation):
    inv_root = 1.0 / math.sqrt(D)
    cent_full = centroids.astype(jnp.float32)
    cent_square = lax.optimization_barrier(jnp.sum(cent_full * cent_full, axis=1))
    row_blocks = vectors.reshape(N_DP, TOK_DEV, D)

    def fold_block(running, row_block):
        sum_rows, soft_mass = running
        cross_dot = lax.dot_general(row_block, centroids, (((1,), (1,)), ((), ())), preferred_element_type=jnp.float32)
        scores = (2.0 * cross_dot - cent_square[None, :]) * inv_root
        peak_val = lax.optimization_barrier(jnp.max(scores, axis=1))
        exp_scores = jnp.exp(scores - peak_val[:, None])
        row_total = lax.optimization_barrier(jnp.sum(exp_scores, axis=1))
        member_prob = (exp_scores / row_total[:, None]).astype(jnp.bfloat16)
        sum_rows = sum_rows + lax.dot_general(member_prob, row_block, (((0,), (0,)), ((), ())), preferred_element_type=jnp.float32)
        soft_mass = soft_mass + lax.optimization_barrier(jnp.sum(member_prob.astype(jnp.float32), axis=0))
        return ((sum_rows, soft_mass), None)
    start_state = (jnp.zeros((K, D), jnp.float32), jnp.zeros((K,), jnp.float32))
    (sum_rows, soft_mass), _ = lax.scan(fold_block, start_state, row_blocks)
    updated = (prior_mass[:, None] * cent_full + sum_rows) / (prior_mass + soft_mass)[:, None]
    new_centroids = updated.reshape(N_CENT, KC, D)
    residual = (vectors.astype(jnp.float32) - cent_full[assign]).astype(jnp.bfloat16)
    rotated = jnp.dot(residual, rotation, preferred_element_type=jnp.float32).astype(jnp.bfloat16)
    owners = owner_of[assign]
    flat_rows = rotated.astype(jnp.float32).reshape(N, M, D // M)

    def owner_moments(owner_idx):
        weight = (owners == owner_idx).astype(jnp.float32)
        return jnp.einsum('r,rmi,rmj->imj', weight, flat_rows, flat_rows).reshape(D // M, D) / TOK_DEV
    moments = lax.map(owner_moments, jnp.arange(N_DP, dtype=jnp.int32))
    return (new_centroids, moments)
```

```python
import functools
import math

import jax
import jax.numpy as jnp
from jax import lax
from jax.experimental import pallas as pl
from jax.experimental.pallas import tpu as pltpu
from jax.sharding import Mesh
from jax.sharding import PartitionSpec as P

F32 = jnp.float32
BF16 = jnp.bfloat16
DP = ("dp_0", "dp_1", "dp_2")
NX, NZ, NC, NY = 4, 8, 2, 8
OWN = 16
SUBS = 48
WIDTHS = (256, 256, 256, 128)


def dot(a, b, dims=((1,), (0,))):
    return lax.dot_general(a, b, (dims, ((), ())), preferred_element_type=F32)


def kernel(
    vec_hbm, cent_hbm, rot_hbm, assign_ref, owner_ref, out_ref,
    vec, cent, rot, score, prob, extra, stat_out, stat_in, rows_out, rows_in,
    own0, own1, own2, own3, snd0, snd1, snd2, snd3, rcv0, rcv1, rcv2, rcv3,
    xs0, xs1, xs2, xs3, xr0, xr1, xr2, xr3,
    zs0, zs1, zs2, zs3, zr0, zr1, zr2, zr3,
    load_sem, stat_ss, stat_rs, rows_ss, rows_rs, core_ss, core_rs, x_ss, x_rs, z_ss, z_rs,
):
    own, snd, rcv = (own0, own1, own2, own3), (snd0, snd1, snd2, snd3), (rcv0, rcv1, rcv2, rcv3)
    xs, xr = (xs0, xs1, xs2, xs3), (xr0, xr1, xr2, xr3)
    zs, zr = (zs0, zs1, zs2, zs3), (zr0, zr1, zr2, zr3)
    px, pz, pc = (lax.axis_index(name) for name in DP)
    py = lax.axis_index("cent")
    rows, width = vec.shape
    per_shard = rows // NY
    inv_root = 1.0 / math.sqrt(width)

    loads = [
        pltpu.make_async_copy(src, dst, load_sem.at[k])
        for k, (src, dst) in enumerate(((vec_hbm, vec), (cent_hbm, cent), (rot_hbm, rot)))
    ]
    for load in loads:
        load.start()

    barrier = pltpu.get_barrier_semaphore()
    partners = [{"cent": lax.rem(py + j, NY)} for j in range(1, NY)]
    partners += [{"dp_2": lax.rem(pc + 1, NC)}]
    partners += [{"dp_0": lax.rem(px + j, NX)} for j in (1, NX - 1)]
    partners += [{"dp_1": lax.rem(pz + j, NZ)} for j in (1, NZ - 1)]
    for partner in partners:
        pl.semaphore_signal(
            barrier, inc=1, device_id=partner, device_id_type=pl.DeviceIdType.MESH
        )

    def remote(src, dst, ss, rs, device):
        return pltpu.make_async_remote_copy(
            src_ref=src, dst_ref=dst, send_sem=ss, recv_sem=rs,
            device_id=device, device_id_type=pl.DeviceIdType.MESH,
        )

    loads[0].wait()
    loads[1].wait()

    tile = 256

    def score_tile(t, top):
        rc = t // 2
        blocks = []
        for step in range(2):
            rx = lax.rem(t, 2) * 2 + step
            for rz in range(NZ):
                blocks.append(
                    cent[lax.rem(px + rx, NX), lax.rem(pz + rz, NZ), lax.rem(pc + rc, NC)]
                )
        lhs = jnp.concatenate(blocks, axis=0)
        wide = lhs.astype(F32)
        square = jnp.sum(wide * wide, axis=1, keepdims=True)
        got = (2.0 * dot(lhs, vec[...], ((1,), (1,))) - square) * inv_root
        score[pl.ds(pl.multiple_of(t * tile, tile), tile), :] = got
        return jnp.maximum(top, jnp.max(got.reshape(tile // 8, 8, rows), axis=0))

    top = lax.fori_loop(0, 4, score_tile, jnp.full((8, rows), -jnp.inf, F32))
    top = jnp.max(top, axis=0, keepdims=True)

    def exp_tile(t, total):
        at = pl.ds(pl.multiple_of(t * 128, 128), 128)
        got = jnp.exp(score[at, :] - top)
        score[at, :] = got
        return total + jnp.sum(got.reshape(16, 8, rows), axis=0)

    total = lax.fori_loop(0, 8, exp_tile, jnp.zeros((8, rows), F32))
    total = jnp.sum(total, axis=0, keepdims=True)
    for j in range(8):
        stat_out[j : j + 1, :] = top[:, 128 * j : 128 * (j + 1)]
        stat_out[8 + j : 9 + j, :] = total[:, 128 * j : 128 * (j + 1)]

    pl.semaphore_wait(barrier, len(partners))
    stat_copies = [
        remote(stat_out, stat_in.at[j - 1], stat_ss.at[j - 1], stat_rs.at[j - 1],
               {"cent": lax.rem(py + j, NY)})
        for j in range(1, NY)
    ]
    for copy in stat_copies:
        copy.start()

    lists = assign_ref[...]
    inside = lax.shift_right_logical(lists, 10) == py
    flag = inside.astype(F32).astype(BF16)
    lane_r = lax.broadcasted_iota(jnp.int32, (128, 128), 0)
    lane_c = lax.broadcasted_iota(jnp.int32, (128, 128), 1)
    before = dot(flag, (lane_r < lane_c).astype(F32).astype(BF16))
    whole = dot(flag, jnp.ones((128, 128), BF16)).astype(BF16)
    sub_r = lax.broadcasted_iota(jnp.int32, (8, 8), 0)
    sub_c = lax.broadcasted_iota(jnp.int32, (8, 8), 1)
    earlier = dot((sub_c < sub_r).astype(F32).astype(BF16), whole)
    rank = jnp.where(inside, before + earlier, -1.0)
    local = jnp.bitwise_and(lists, 1023).astype(F32)
    holder = owner_ref[py].astype(F32)

    def as_row(a):
        return jnp.concatenate([a[j : j + 1, :] for j in range(8)], axis=1)

    slot = lax.broadcasted_iota(jnp.int32, (per_shard, rows), 0).astype(F32)
    place = lax.broadcasted_iota(jnp.int32, (per_shard, rows), 1).astype(F32)
    pick = slot == as_row(rank)
    list_of = jnp.sum(jnp.where(pick, as_row(local), 0.0), axis=1, keepdims=True)
    member = place == list_of
    owner_col = jnp.sum(jnp.where(member, as_row(holder), 0.0), axis=1, keepdims=True)
    vec_rows = dot(pick.astype(F32).astype(BF16), vec[...])
    cent_rows = dot(member.astype(F32).astype(BF16), cent[...].reshape(rows, width))
    residual = (vec_rows - cent_rows).astype(BF16)
    loads[2].wait()
    turned = dot(residual, rot[...])
    span = width // NY
    pad = jnp.broadcast_to(owner_col, (per_shard, 128 - span))
    for c in range(NY):
        rows_out[c] = jnp.concatenate(
            [turned[:, span * c : span * (c + 1)], pad], axis=1
        ).astype(BF16)
    row_copies = [
        remote(rows_out.at[lax.rem(py + j, NY)], rows_in.at[j - 1],
               rows_ss.at[j - 1], rows_rs.at[j - 1], {"cent": lax.rem(py + j, NY)})
        for j in range(1, NY)
    ]
    for copy in row_copies:
        copy.start()

    for copy in stat_copies:
        copy.wait_recv()
    own_top, own_total = stat_out[0:8, :], stat_out[8:16, :]
    peak = own_top
    for j in range(NY - 1):
        peak = jnp.maximum(peak, stat_in[j, 0:8, :])
    scale = jnp.exp(own_top - peak)
    whole_total = own_total * scale
    for j in range(NY - 1):
        whole_total += stat_in[j, 8:16, :] * jnp.exp(stat_in[j, 0:8, :] - peak)
    factor = as_row(scale / whole_total)

    def prob_tile(t, carry):
        at = pl.ds(pl.multiple_of(t * 128, 128), 128)
        got = (score[at, :] * factor).astype(BF16)
        prob[at, :] = got
        mass = jnp.sum(got.astype(F32), axis=1, keepdims=True)
        high = mass.astype(BF16).astype(F32)
        lane = lax.broadcasted_iota(jnp.int32, (128, 128), 1)
        extra[at, :] = jnp.where(lane == 96, high, jnp.where(lane == 97, mass - high, 0.0))
        return carry

    lax.fori_loop(0, 8, prob_tile, 0)

    half = rows // 2
    sibling = {"dp_2": lax.rem(pc + 1, NC)}
    x_up, x_down = {"dp_0": lax.rem(px + 1, NX)}, {"dp_0": lax.rem(px + NX - 1, NX)}
    z_up, z_down = {"dp_1": lax.rem(pz + 1, NZ)}, {"dp_1": lax.rem(pz + NZ - 1, NZ)}
    core_copies = [
        remote(snd[c], rcv[c], core_ss.at[c], core_rs.at[c], sibling) for c in range(4)
    ]

    def x_copy(c, step, side):
        size = 64 if step == 0 else 128
        k = (c * 2 + step) * 2 + side
        at = pl.ds(0 if step == 0 else 64, size)
        return remote(xs[c].at[side, at], xr[c].at[side, at], x_ss.at[k], x_rs.at[k],
                      (x_up, x_down)[side])

    def z_copy(c, step, side):
        k = (c * 4 + step) * 2 + side
        size = 8 if step == 0 else 16
        at = pl.ds(0, size)
        return remote(zs[c].at[step, side, at], zr[c].at[step, side, at],
                      z_ss.at[k], z_rs.at[k], (z_up, z_down)[side])

    def stage_a(c):
        columns = vec[:, 256 * c : 256 * (c + 1)]
        snd[c][...] = dot(prob[half:, :], columns).astype(BF16)
        core_copies[c].start()
        own[c][...] = dot(prob[:half, :], columns)

    def stage_moments():
        for copy in row_copies:
            copy.wait_recv()
        got = jnp.concatenate([rows_out[py]] + [rows_in[j] for j in range(NY - 1)], axis=0)
        mine = got[:, 96:97].astype(F32)
        q = lax.broadcasted_iota(jnp.int32, (rows, 64), 1)
        qc, qx, qz = q // 32, (q // 8) % 4, q % 8
        wanted = (((px + qx) % NX) * NZ + (pz + qz) % NZ) * NC + (pc + qc) % NC
        chosen = (wanted.astype(F32) == mine).astype(F32).astype(BF16)
        from_lane = lax.broadcasted_iota(jnp.int32, (128, 256), 0)
        to_lane = lax.broadcasted_iota(jnp.int32, (128, 256), 1)
        twice = got.astype(F32)
        twice = jnp.concatenate([twice, twice], axis=1)
        ones = jnp.ones((1, 1), F32)
        keep = lax.broadcasted_iota(jnp.int32, (64, 128), 1) < 96
        for pair in range(8):
            source = (to_lane % 128) // 16 * 16 + 2 * pair + to_lane // 128
            spread = dot(got, (from_lane == source).astype(F32).astype(BF16))
            both = dot(chosen, (spread * twice).astype(BF16), ((0,), (0,)))
            for side in range(2):
                part = jnp.where(keep, both[:, 128 * side : 128 * (side + 1)], 0.0)
                a = 2 * pair + side
                moment = extra.reshape(64, OWN, 128)
                moment[:, a, :] = moment[:, a, :] + part
        snd[3][...] = extra[half:, :].astype(BF16)
        core_copies[3].start()
        own[3][...] = extra[:half, :]

    def stage_b(c):
        core_copies[c].wait_recv()
        far = own[c][256:384, :] + rcv[c][256:384, :].astype(F32)
        xs[c][0, 0:64] = far[0:64].astype(BF16)
        xs[c][1, 0:64] = far[64:128].astype(BF16)
        for side in range(2):
            x_copy(c, 0, side).start()
        for at in (slice(0, 256), slice(384, 512)):
            own[c][at, :] = own[c][at, :] + rcv[c][at, :].astype(F32)

    def stage_c(c):
        for side in range(2):
            x_copy(c, 0, side).wait_recv()
        xs[c][0, 64:128] = (own[c][128:192, :] + xr[c][0, 0:64].astype(F32)).astype(BF16)
        xs[c][0, 128:192] = own[c][192:256, :].astype(BF16)
        xs[c][1, 64:128] = own[c][384:448, :].astype(BF16)
        xs[c][1, 128:192] = (own[c][448:512, :] + xr[c][1, 0:64].astype(F32)).astype(BF16)
        for side in range(2):
            x_copy(c, 1, side).start()

    def stage_d(c):
        for side in range(2):
            x_copy(c, 1, side).wait_recv()
        own[c][0:128, :] = (
            own[c][0:128, :]
            + xr[c][0, 64:192].astype(F32)
            + xr[c][1, 64:192].astype(F32)
        )
        zs[c][0, 0, 0:8] = own[c][64:72, :]
        zs[c][0, 1, 0:8] = own[c][72:80, :]
        for side in range(2):
            z_copy(c, 0, side).start()

    def stage_z(c, step):
        for side in range(2):
            z_copy(c, step - 1, side).wait_recv()
        up, down = 16 * (4 - step), 16 * (4 + step)
        if step == 1:
            zs[c][1, 0, 0:8] = own[c][up : up + 8, :] + zr[c][0, 0, 0:8]
            zs[c][1, 0, 8:16] = own[c][up + 8 : up + 16, :]
            zs[c][1, 1, 0:8] = own[c][down : down + 8, :]
            zs[c][1, 1, 8:16] = own[c][down + 8 : down + 16, :] + zr[c][0, 1, 0:8]
        else:
            zs[c][step, 0] = own[c][up : up + 16, :] + zr[c][step - 1, 0]
            zs[c][step, 1] = own[c][down : down + 16, :] + zr[c][step - 1, 1]
        for side in range(2):
            z_copy(c, step, side).start()

    def stage_end(c):
        for side in range(2):
            z_copy(c, 3, side).wait_recv()
        at = 256 * c
        out_ref[:, at : at + WIDTHS[c]] = own[c][0:16, :] + zr[c][3, 0] + zr[c][3, 1]

    stages = [
        lambda c: stage_a(c) if c < 3 else stage_moments(),
        stage_b, stage_c, stage_d,
        lambda c: stage_z(c, 1), lambda c: stage_z(c, 2), lambda c: stage_z(c, 3),
        stage_end,
    ]
    for wave in range(len(stages) + 3):
        for c in range(4):
            if 0 <= wave - c < len(stages):
                stages[wave - c](c)

    for copy in stat_copies + row_copies + core_copies:
        copy.wait_send()
    for c in range(4):
        for side in range(2):
            for step in range(2):
                x_copy(c, step, side).wait_send()
            for step in range(4):
                z_copy(c, step, side).wait_send()


def body(vectors, centroids, prior_mass, assign, owner_of, rotation):
    rows, width = vectors.shape
    dp_pos = lax.axis_index(DP)
    own_count = centroids.shape[0] // (NX * NZ * NC)
    half = rows // 2
    any_spec = pl.BlockSpec(memory_space=pl.ANY)
    vmem_spec = pl.BlockSpec(memory_space=pltpu.VMEM)
    dma = pltpu.SemaphoreType.DMA
    scratch = [
        pltpu.VMEM((rows, width), BF16),
        pltpu.VMEM((NX, NZ, NC, OWN, width), BF16),
        pltpu.VMEM((width, width), BF16),
        pltpu.VMEM((rows, rows), F32),
        pltpu.VMEM((rows, rows), BF16),
        pltpu.VMEM((rows, 128), F32),
        pltpu.VMEM((16, 128), F32),
        pltpu.VMEM((NY - 1, 16, 128), F32),
        pltpu.VMEM((NY, 128, 128), BF16),
        pltpu.VMEM((NY - 1, 128, 128), BF16),
    ]
    scratch += [pltpu.VMEM((half, w), F32) for w in WIDTHS]
    scratch += [pltpu.VMEM((half, w), BF16) for w in WIDTHS] * 2
    scratch += [pltpu.VMEM((2, 192, w), BF16) for w in WIDTHS] * 2
    scratch += [pltpu.VMEM((4, 2, 16, w), F32) for w in WIDTHS] * 2
    scratch += [dma((3,))] + [dma((7,))] * 4 + [dma((4,))] * 2 + [dma((16,))] * 2 + [dma((32,))] * 2
    got = pl.pallas_call(
        kernel,
        out_shape=jax.ShapeDtypeStruct((OWN, sum(WIDTHS)), F32),
        in_specs=[any_spec] * 3 + [vmem_spec] * 2,
        out_specs=vmem_spec,
        scratch_shapes=scratch,
        compiler_params=pltpu.CompilerParams(
            collective_id=0, has_side_effects=True, vmem_limit_bytes=48 * 1024 * 1024
        ),
    )(
        vectors,
        centroids.reshape(NX, NZ, NC, OWN, width),
        rotation,
        assign.reshape(8, 128),
        owner_of.reshape(NY, 8, 128),
    )
    own_sums = got[:, :width]
    own_mass = got[:, width + 96] + got[:, width + 97]
    own_cent = lax.dynamic_slice_in_dim(centroids, dp_pos * own_count, own_count, 0).astype(F32)
    own_prior = lax.dynamic_slice_in_dim(prior_mass, dp_pos * own_count, own_count, 0)
    updated = (own_prior[:, None] * own_cent + own_sums) / (own_prior + own_mass)[:, None]
    moments = got[:, width : width + 96] / rows
    return (updated[None], moments[None])


def solution(mesh):
    finer = Mesh(
        mesh.devices.reshape(NX, NZ, NC, mesh.shape["cent"]), ("dp_0", "dp_1", "dp_2", "cent")
    )
    in_specs = (P(DP, None), P("cent", None), P("cent"), P(DP), P(), P())
    out_specs = (P("cent", DP, None), P(DP, None, "cent"))
    return jax.shard_map(body, mesh=finer, in_specs=in_specs, out_specs=out_specs, check_vma=False)
```

```python
import contextlib
import math

import jax
import jax.numpy as jnp
from jax import lax
from jax.experimental import pallas as pl
from jax.experimental.pallas import tpu as pltpu
from jax.sharding import Mesh
from jax.sharding import PartitionSpec as P

F32 = jnp.float32
BF16 = jnp.bfloat16
DP = ("dp_0", "dp_1", "dp_2")
NX, NZ, NC, NY = 4, 8, 2, 8
OWN = 16
SUB = 16
WIDTHS = (384, 384, 128)
scope = contextlib.nullcontext


def dot(a, b, dims=((1,), (0,))):
    return lax.dot_general(a, b, (dims, ((), ())), preferred_element_type=F32)


def as_row(a):
    return jnp.concatenate([a[j : j + 1, :] for j in range(a.shape[0])], axis=1)


def as_bf16(mask):
    return mask.astype(F32).astype(BF16)


def iota(shape, dim):
    return lax.broadcasted_iota(jnp.int32, shape, dim)


def kernel(
    vec_hbm, cent_hbm, rot_hbm, prior_hbm, assign_hbm, owner_hbm, new_ref, mom_ref,
    vec, cent, rot, prior, assign, owner, score, prob, weight, moment,
    stat_out, stat_in, rows_out, rows_in, turned_rows,
    own0, own1, own2, snd0, snd1, snd2, rcv0, rcv1, rcv2,
    xs0, xs1, xr0, xr1, zs0, zs1, zs2, zr0, zr1, zr2, last, last_in,
    load_sem, stat_ss, stat_rs, rows_ss, rows_rs, core_ss, core_rs, x_ss, x_rs, z_ss, z_rs,
    last_ss, last_rs,
):
    own, snd, rcv = (own0, own1, own2), (snd0, snd1, snd2), (rcv0, rcv1, rcv2)
    xs, xr, zs, zr = (xs0, xs1), (xr0, xr1), (zs0, zs1, zs2), (zr0, zr1, zr2)
    px, pz, pc = (lax.axis_index(name) for name in DP)
    py = lax.axis_index("cent")
    rows, width = vec.shape
    per_shard = rows // NY
    span = width // NY
    inv_root = 1.0 / math.sqrt(width)

    def load(k, src, dst):
        return pltpu.make_async_copy(src, dst, load_sem.at[k])

    vec_loads = [
        load(9 + k, vec_hbm.at[pl.ds(256 * k, 256)], vec.at[pl.ds(256 * k, 256)]) for k in range(4)
    ]
    cent_loads = [
        load(1 + k, cent_hbm.at[lax.rem(px + k, NX)], cent.at[lax.rem(px + k, NX)])
        for k in range(NX)
    ]
    small_loads = [
        load(5, assign_hbm, assign), load(6, owner_hbm.at[py], owner), load(7, prior_hbm, prior)
    ]
    rot_load = load(8, rot_hbm, rot)
    for item in vec_loads + cent_loads:
        item.start()

    barrier = pltpu.get_barrier_semaphore()
    partners = [{"cent": lax.rem(py + j, NY)} for j in range(1, NY)]
    partners += [{"dp_2": lax.rem(pc + 1, NC)}]
    partners += [{"dp_0": lax.rem(px + j, NX)} for j in range(1, NX)]
    partners += [{"dp_1": lax.rem(pz + j, NZ)} for j in range(1, NZ)]
    for partner in partners:
        pl.semaphore_signal(
            barrier, inc=1, device_id=partner, device_id_type=pl.DeviceIdType.MESH
        )

    def remote(src, dst, ss, rs, device):
        return pltpu.make_async_remote_copy(
            src_ref=src, dst_ref=dst, send_sem=ss, recv_sem=rs,
            device_id=device, device_id_type=pl.DeviceIdType.MESH,
        )

    with scope("loadwait"):
        for item in vec_loads:
            item.wait()
    for item in small_loads + [rot_load]:
        item.start()
    tops = []
    with scope("score"):
        for rx in range(NX):
            cent_loads[rx].wait()
            blocks = [
                cent[lax.rem(px + rx, NX), lax.rem(pz + rz, NZ), lax.rem(pc + rc, NC)]
                for rc in range(NC)
                for rz in range(NZ)
            ]
            lhs = jnp.concatenate(blocks, axis=0)
            wide = lhs.astype(F32)
            square = jnp.sum(wide * wide, axis=1, keepdims=True)
            got = (2.0 * dot(lhs, vec[...], ((1,), (1,))) - square) * inv_root
            top = jnp.max(jnp.max(got.reshape(32, 8, rows), axis=0), axis=0, keepdims=True)
            if rx:
                top = jnp.maximum(top, tops[-1])
            got = jnp.exp(got - top)
            for rc in range(NC):
                at = 512 * rc + 128 * rx
                score[at : at + 128, :] = got[128 * rc : 128 * (rc + 1)]
            part = jnp.sum(got.reshape(32, 8, rows), axis=0)
            total = part + total * jnp.exp(tops[-1] - top) if rx else part
            tops.append(top)
    level = tops[-1] + jnp.log(jnp.sum(total, axis=0, keepdims=True))
    for j in range(8):
        stat_out[j : j + 1, :] = level[:, 128 * j : 128 * (j + 1)]

    with scope("barrier"):
        pl.semaphore_wait(barrier, len(partners))
    stat_copies = [
        remote(stat_out, stat_in.at[j - 1], stat_ss.at[j - 1], stat_rs.at[j - 1],
               {"cent": lax.rem(py + j, NY)})
        for j in range(1, NY)
    ]
    for copy in stat_copies:
        copy.start()

    with scope("rows"):
        for item in small_loads:
            item.wait()
        lists = assign[...]
        inside = lax.shift_right_logical(lists, 10) == py
        flag = as_bf16(inside)
        before = dot(flag, as_bf16(iota((128, 128), 0) < iota((128, 128), 1)))
        whole = dot(flag, jnp.ones((128, 128), BF16)).astype(BF16)
        earlier = dot(as_bf16(iota((8, 8), 1) < iota((8, 8), 0)), whole)
        rank = jnp.where(inside, before + earlier, -1.0)
        local = jnp.bitwise_and(lists, 1023).astype(F32)
        pick = iota((per_shard, rows), 0).astype(F32) == as_row(rank)
        list_of = jnp.sum(jnp.where(pick, as_row(local), 0.0), axis=1, keepdims=True)
        member = iota((per_shard, rows), 1).astype(F32) == list_of
        holder = as_row(owner[...].astype(F32))
        owner_col = jnp.sum(jnp.where(member, holder, 0.0), axis=1, keepdims=True)
        vec_rows = dot(as_bf16(pick), vec[...])
        cent_rows = dot(as_bf16(member), cent[...].reshape(rows, width))
        residual = (vec_rows - cent_rows).astype(BF16)
        rot_load.wait()
        turned = dot(residual, rot[...])
        owner_wide = jnp.broadcast_to(owner_col, (per_shard, 128))
        turned = jnp.concatenate([turned, owner_wide], axis=1).T.astype(BF16)
        for c in range(NY):
            rows_out[c, 0:span] = turned[span * c : span * (c + 1)]
            rows_out[c, span : span + 16] = turned[width : width + 16]
    row_copies = [
        remote(rows_out.at[lax.rem(py + j, NY)], rows_in.at[j - 1],
               rows_ss.at[j - 1], rows_rs.at[j - 1], {"cent": lax.rem(py + j, NY)})
        for j in range(1, NY)
    ]
    for copy in row_copies:
        copy.start()

    with scope("statwait"):
        for copy in stat_copies:
            copy.wait_recv()
    levels = [stat_out[...]] + [stat_in[j] for j in range(NY - 1)]
    peak = levels[0]
    for item in levels[1:]:
        peak = jnp.maximum(peak, item)
    whole_total = jnp.exp(levels[0] - peak)
    for item in levels[1:]:
        whole_total += jnp.exp(item - peak)
    peak, whole_total = as_row(peak), as_row(whole_total)

    sibling = {"dp_2": lax.rem(pc + 1, NC)}
    x_side = [{"dp_0": lax.rem(px + j, NX)} for j in (1, NX - 1)]

    def core_copy(q, rx):
        k = q * NX + rx
        at = pl.ds(128 * rx, 128)
        return remote(snd[q].at[at], rcv[q].at[at], core_ss.at[k], core_rs.at[k], sibling)

    moment_copy = remote(snd[2], rcv[2], core_ss.at[8], core_rs.at[8], sibling)

    def x_copy(q, j):
        k = q * 6 + j
        return remote(xs[q].at[j], xr[q].at[j], x_ss.at[k], x_rs.at[k], x_side[j % 2])

    def z_copy(q, j):
        k = q * (NZ - 1) + j - 1
        return remote(zs[q].at[j - 1], zr[q].at[j - 1], z_ss.at[k], z_rs.at[k],
                      {"dp_1": lax.rem(pz + j, NZ)})

    def last_copy(j):
        return remote(last.at[j], last_in.at[j - 1], last_ss.at[j - 1], last_rs.at[j - 1],
                      {"dp_0": lax.rem(px + j, NX)})

    def sums(rx):
        at, sent = slice(128 * rx, 128 * (rx + 1)), slice(512 + 128 * rx, 640 + 128 * rx)
        factor = jnp.exp(tops[rx] - peak) / whole_total
        for side in (sent, at):
            got = score[side, :] * factor
            prob[side, :] = got.astype(BF16)
            parts = [got[:, 128 * j : 128 * (j + 1)] for j in range(8)]
            while len(parts) > 1:
                parts = [a + b for a, b in zip(parts[::2], parts[1::2])]
            weight[side, :] = parts[0]
        got = dot(jnp.concatenate([prob[sent, :], prob[at, :]], axis=0), vec[...])
        for q in range(2):
            snd[q][at, :] = got[:128, 384 * q : 384 * (q + 1)].astype(BF16)
            core_copy(q, rx).start()
        for q in range(2):
            own[q][at, :] = got[128:, 384 * q : 384 * (q + 1)]

    def split_mass(a):
        lane = iota(a.shape, 1)
        mass = jnp.where((lane >= span) & (lane < span + 2), a, 0.0)
        mass = jnp.sum(mass, axis=1, keepdims=True)
        high = mass.astype(BF16).astype(F32)
        return jnp.where(lane == span, high, jnp.where(lane == span + 1, mass - high, a))

    def moments():
        for copy in row_copies:
            copy.wait_recv()
        got = jnp.concatenate([rows_out[py]] + [rows_in[j] for j in range(NY - 1)], axis=1)
        turned_rows[...] = got[0:span].astype(F32)
        holders = got[span : span + 1].astype(F32)
        q = iota((64, 1), 0)
        qc, qx, qz = q // 32, (q // 8) % 4, q % 8
        wanted = (((px + qx) % NX) * NZ + (pz + qz) % NZ) * NC + (pc + qc) % NC
        chosen = as_bf16(wanted.astype(F32) == holders)
        filler = jnp.zeros((128 - span, rows), BF16)
        by_owner = moment.reshape(64, OWN, 128)
        for pair in range(SUB // 2):
            pieces = []
            for a in (2 * pair, 2 * pair + 1):
                for m in range(span // SUB):
                    block = turned_rows[SUB * m : SUB * (m + 1), :]
                    line = turned_rows[SUB * m + a : SUB * m + a + 1, :]
                    pieces.append((block * line).astype(BF16))
                pieces.append(filler)
            both = dot(chosen, jnp.concatenate(pieces, axis=0), ((1,), (1,)))
            for side in range(2):
                by_owner[:, 2 * pair + side, :] = both[:, 128 * side : 128 * (side + 1)]
        mass = jnp.sum(weight[...], axis=1, keepdims=True)
        both = split_mass(moment[...] + jnp.where(iota((rows, 128), 1) == span, mass, 0.0))
        snd[2][...] = both[512:].astype(BF16)
        moment_copy.start()
        own[2][...] = both[:512]

    def joined(q, rx):
        core_copy(q, rx).wait_recv()
        at = slice(128 * rx, 128 * (rx + 1))
        return own[q][at, :] + rcv[q][at, :].astype(F32)

    def x_far(q):
        got = joined(q, 2).astype(BF16)
        for side in range(2):
            xs[q][side] = got[64 * side : 64 * (side + 1)]
            x_copy(q, side).start()

    def x_plain(q, side):
        got = joined(q, (1, 3)[side])
        plain, rest = (got[64:], got[:64]) if side == 0 else (got[:64], got[64:])
        xs[q][2 + side] = plain.astype(BF16)
        x_copy(q, 2 + side).start()
        own[q][128 * (1 + side) : 128 * (1 + side) + 64, :] = rest

    def x_add(q):
        for side in range(2):
            x_copy(q, side).wait_recv()
            rest = own[q][128 * (1 + side) : 128 * (1 + side) + 64, :]
            xs[q][4 + side] = (rest + xr[q][side].astype(F32)).astype(BF16)
            x_copy(q, 4 + side).start()

    def near(q):
        own[q][0:128, :] = joined(q, 0)

    def z_send(q):
        for j in (2, 3, 4, 5):
            x_copy(q, j).wait_recv()
        low = own[q][0:64, :] + xr[q][4].astype(F32) + xr[q][3].astype(F32)
        high = own[q][64:128, :] + xr[q][2].astype(F32) + xr[q][5].astype(F32)
        block = [part[16 * j : 16 * (j + 1)] for part in (low, high) for j in range(4)]
        for j in (4, 3, 5, 2, 6, 1, 7):
            zs[q][j - 1] = block[j].astype(BF16)
            z_copy(q, j).start()
        own[q][0:OWN, :] = block[0]

    def finish(q):
        got = own[q][0:OWN, :]
        for j in (1, 7, 2, 6, 3, 5, 4):
            z_copy(q, j).wait_recv()
            got = got + zr[q][j - 1].astype(F32)
        return got

    def moments_z():
        moment_copy.wait_recv()
        got = split_mass(own[2][...] + rcv[2][...].astype(F32)).reshape(NX, NZ, OWN, 128)
        for j in (4, 3, 5, 2, 6, 1, 7):
            zs[2][j - 1] = got[:, j].astype(BF16)
            z_copy(2, j).start()
        last[...] = got[:, 0]

    def moments_x():
        got = last[...]
        for j in (1, 7, 2, 6, 3, 5, 4):
            z_copy(2, j).wait_recv()
            got = got + zr[2][j - 1].astype(F32)
        last[...] = got
        for j in (2, 1, 3):
            last_copy(j).start()

    def moments_end():
        got = last[0]
        for j in range(1, NX):
            last_copy(j).wait_recv()
            got = got + last_in[j - 1]
        return got

    def staged(stage, *at):
        with scope(stage.__name__ + "".join(map(str, at))):
            return stage(*at)

    staged(sums, 2)
    staged(sums, 1)
    staged(x_far, 0)
    staged(x_far, 1)
    staged(sums, 3)
    staged(x_plain, 0, 0)
    staged(x_plain, 1, 0)
    staged(sums, 0)
    staged(x_plain, 0, 1)
    staged(x_plain, 1, 1)
    staged(moments)
    staged(near, 0)
    staged(near, 1)
    staged(x_add, 0)
    staged(x_add, 1)
    staged(moments_z)
    staged(z_send, 0)
    staged(z_send, 1)
    staged(moments_x)
    parts = [staged(finish, 0), staged(finish, 1), staged(moments_end)]
    lane = iota((OWN, 128), 1)
    mass = jnp.sum(
        jnp.where((lane >= span) & (lane < span + 2), parts[2], 0.0), axis=1, keepdims=True
    )
    first = ((px * NZ + pz) * NC + pc) * OWN
    mine = iota((OWN, rows), 1) == iota((OWN, rows), 0) + first
    prior_col = jnp.sum(jnp.where(mine, as_row(prior[...]), 0.0), axis=1, keepdims=True)
    own_cent = cent[px, pz, pc].astype(F32)
    new_ref[...] = (prior_col * own_cent + jnp.concatenate(parts[:2], axis=1)) / (prior_col + mass)
    mom_ref[...] = parts[2][:, :span] / rows

    with scope("endwaits"):
        for copy in stat_copies + row_copies:
            copy.wait_send()
        moment_copy.wait_send()
        for q in range(2):
            for rx in range(NX):
                core_copy(q, rx).wait_send()
            for j in range(6):
                x_copy(q, j).wait_send()
        for j in range(1, NX):
            last_copy(j).wait_send()
        for q in range(3):
            for j in range(1, NZ):
                z_copy(q, j).wait_send()


def body(vectors, centroids, prior_mass, assign, owner_of, rotation):
    rows, width = vectors.shape
    span = width // NY
    half = rows // 2
    any_spec = pl.BlockSpec(memory_space=pl.ANY)
    vmem_spec = pl.BlockSpec(memory_space=pltpu.VMEM)
    dma = pltpu.SemaphoreType.DMA
    scratch = [
        pltpu.VMEM((rows, width), BF16),
        pltpu.VMEM((NX, NZ, NC, OWN, width), BF16),
        pltpu.VMEM((width, width), BF16),
        pltpu.VMEM((8, 128), F32),
        pltpu.VMEM((8, 128), jnp.int32),
        pltpu.VMEM((8, 128), jnp.int32),
        pltpu.VMEM((rows, rows), F32),
        pltpu.VMEM((rows, rows), BF16),
        pltpu.VMEM((rows, 128), F32),
        pltpu.VMEM((rows, 128), F32),
        pltpu.VMEM((8, 128), F32),
        pltpu.VMEM((NY - 1, 8, 128), F32),
        pltpu.VMEM((NY, span + 16, 128), BF16),
        pltpu.VMEM((NY - 1, span + 16, 128), BF16),
        pltpu.VMEM((span, rows), F32),
    ]
    scratch += [pltpu.VMEM((half, w), F32) for w in WIDTHS]
    scratch += [pltpu.VMEM((half, w), BF16) for w in WIDTHS] * 2
    scratch += [pltpu.VMEM((6, 64, w), BF16) for w in WIDTHS[:2]] * 2
    turns = [pltpu.VMEM((NZ - 1, OWN, w), BF16) for w in WIDTHS[:2]]
    turns += [pltpu.VMEM((NZ - 1, NX, OWN, 128), BF16)]
    scratch += turns * 2 + [pltpu.VMEM((NX, OWN, 128), F32), pltpu.VMEM((NX - 1, OWN, 128), F32)]
    scratch += [dma((13,))] + [dma((7,))] * 4 + [dma((9,))] * 2 + [dma((12,))] * 2 + [dma((21,))] * 2
    scratch += [dma((3,))] * 2
    updated, moments = pl.pallas_call(
        kernel,
        out_shape=(
            jax.ShapeDtypeStruct((OWN, width), F32),
            jax.ShapeDtypeStruct((OWN, span), F32),
        ),
        in_specs=[any_spec] * 6,
        out_specs=(vmem_spec, vmem_spec),
        scratch_shapes=scratch,
        compiler_params=pltpu.CompilerParams(
            collective_id=0, has_side_effects=True, vmem_limit_bytes=40000 * 1024
        ),
    )(*(pltpu.with_memory_space_constraint(a, pltpu.HBM) for a in (
        vectors,
        centroids.reshape(NX, NZ, NC, OWN, width),
        rotation,
        prior_mass.reshape(8, 128),
        assign.reshape(8, 128),
        owner_of.reshape(NY, 8, 128),
    )))
    return (updated[None], moments[None])


def solution(mesh):
    finer = Mesh(
        mesh.devices.reshape(NX, NZ, NC, mesh.shape["cent"]), ("dp_0", "dp_1", "dp_2", "cent")
    )
    in_specs = (P(DP, None), P("cent", None), P("cent"), P(DP), P(), P())
    out_specs = (P("cent", DP, None), P(DP, None, "cent"))
    return jax.shard_map(body, mesh=finer, in_specs=in_specs, out_specs=out_specs, check_vma=False)
```

```python
import contextlib
import math

import jax
import jax.numpy as jnp
from jax import lax
from jax.experimental import pallas as pl
from jax.experimental.pallas import tpu as pltpu
from jax.sharding import Mesh
from jax.sharding import PartitionSpec as P

F32 = jnp.float32
BF16 = jnp.bfloat16
DP = ("dp_0", "dp_1", "dp_2")
NX, NZ, NC, NY = 4, 8, 2, 8
OWN = 16
SUB = 16
scope = contextlib.nullcontext


def dot(a, b, dims=((1,), (0,))):
    return lax.dot_general(a, b, (dims, ((), ())), preferred_element_type=F32)


def as_row(a):
    return jnp.concatenate([a[j : j + 1, :] for j in range(a.shape[0])], axis=1)


def as_bf16(mask):
    return mask.astype(F32).astype(BF16)


def iota(shape, dim):
    return lax.broadcasted_iota(jnp.int32, shape, dim)


def kernel(
    vec_hbm, cent_hbm, rot_hbm, prior_hbm, assign_hbm, owner_hbm, new_ref, mom_ref,
    vec, cent, rot, prior, assign, owner, score, prob, weight, moment,
    stat_out, stat_in, rows_out, rows_in, turned_rows,
    own, own_m, snd, snd_m, rcv, rcv_m,
    xs0, xs1, xr0, xr1, zs0, zs1, zs2, zr0, zr1, zr2, last, last_in,
    load_sem, send_sem, recv_sem,
):
    xs, xr, zs, zr = (xs0, xs1), (xr0, xr1), (zs0, zs1, zs2), (zr0, zr1, zr2)
    px, pz, pc = (lax.axis_index(name) for name in DP)
    py = lax.axis_index("cent")
    rows, width = vec.shape
    per_shard = rows // NY
    span = width // NY
    inv_root = 1.0 / math.sqrt(width)

    def load(k, src, dst):
        return pltpu.make_async_copy(src, dst, load_sem.at[k])

    def wait_all(ref, sem):
        pltpu.make_async_copy(ref, ref, sem).wait()

    cent_loads = [
        load(k, cent_hbm.at[lax.rem(px + k, NX)], cent.at[lax.rem(px + k, NX)])
        for k in range(NX)
    ]
    small_loads = [
        load(5, assign_hbm, assign), load(6, owner_hbm.at[py], owner), load(7, prior_hbm, prior)
    ]
    rot_load = load(8, rot_hbm, rot)
    for k in range(4):
        load(4, vec_hbm.at[pl.ds(256 * k, 256)], vec.at[pl.ds(256 * k, 256)]).start()
    cent_loads[0].start()

    barrier = pltpu.get_barrier_semaphore()
    partners = [{"cent": lax.rem(py + j, NY)} for j in range(1, NY)]
    partners += [{"dp_2": lax.rem(pc + 1, NC)}]
    partners += [{"dp_0": lax.rem(px + j, NX)} for j in range(1, NX)]
    partners += [{"dp_1": lax.rem(pz + j, NZ)} for j in range(1, NZ)]
    for partner in partners:
        pl.semaphore_signal(
            barrier, inc=1, device_id=partner, device_id_type=pl.DeviceIdType.MESH
        )

    for item in cent_loads[1:]:
        item.start()

    def remote(src, dst, ss, rs, device):
        return pltpu.make_async_remote_copy(
            src_ref=src, dst_ref=dst, send_sem=send_sem.at[ss], recv_sem=recv_sem.at[rs],
            device_id=device, device_id_type=pl.DeviceIdType.MESH,
        )

    with scope("loadwait"):
        wait_all(vec, load_sem.at[4])
    for item in small_loads + [rot_load]:
        item.start()
    tops, total = [], None
    with scope("score"):
        cent_loads[0].wait()
        for rx in range(NX + 1):
            if rx < NX:
                blocks = [
                    cent[lax.rem(px + rx, NX), lax.rem(pz + rz, NZ), lax.rem(pc + rc, NC)]
                    for rc in range(NC)
                    for rz in range(NZ)
                ]
                lhs = jnp.concatenate(blocks, axis=0)
                wide = lhs.astype(F32)
                square = jnp.sum(wide * wide, axis=1, keepdims=True)
                got = (2.0 * dot(lhs, vec[...], ((1,), (1,))) - square) * inv_root
                for rc in range(NC):
                    at = 512 * rc + 128 * rx
                    score[at : at + 128, :] = got[128 * rc : 128 * (rc + 1)]
                top = jnp.max(jnp.max(got.reshape(32, 8, rows), axis=0), axis=0, keepdims=True)
                tops.append(jnp.maximum(top, tops[-1]) if rx else top)
            if rx == 0:
                for item in cent_loads[1:]:
                    item.wait()
            else:
                top, part = tops[rx - 1], jnp.zeros((8, rows), F32)
                for rc in range(NC):
                    at = 512 * rc + 128 * (rx - 1)
                    got = jnp.exp(score[at : at + 128, :] - top)
                    score[at : at + 128, :] = got
                    part = part + jnp.sum(got.reshape(16, 8, rows), axis=0)
                total = part + total * jnp.exp(tops[rx - 2] - top) if rx > 1 else part
    level = tops[-1] + jnp.log(jnp.sum(total, axis=0, keepdims=True))
    for j in range(8):
        stat_out[j : j + 1, :] = level[:, 128 * j : 128 * (j + 1)]

    with scope("barrier"):
        pl.semaphore_wait(barrier, len(partners))
    stat_copies = [
        remote(stat_out, stat_in.at[j - 1], 0, 0,
               {"cent": lax.rem(py + j, NY)})
        for j in range(1, NY)
    ]
    for copy in stat_copies:
        copy.start()

    with scope("rows"):
        for item in small_loads:
            item.wait()
        lists = assign[...]
        inside = lax.shift_right_logical(lists, 10) == py
        flag = as_bf16(inside)
        before = dot(flag, as_bf16(iota((128, 128), 0) < iota((128, 128), 1)))
        whole = dot(flag, jnp.ones((128, 128), BF16)).astype(BF16)
        earlier = dot(as_bf16(iota((8, 8), 1) < iota((8, 8), 0)), whole)
        rank = jnp.where(inside, before + earlier, -1.0)
        local = jnp.bitwise_and(lists, 1023).astype(F32)
        pick = iota((per_shard, rows), 0).astype(F32) == as_row(rank)
        list_of = jnp.sum(jnp.where(pick, as_row(local), 0.0), axis=1, keepdims=True)
        member = iota((per_shard, rows), 1).astype(F32) == list_of
        holder = as_row(owner[...].astype(F32))
        owner_col = jnp.sum(jnp.where(member, holder, 0.0), axis=1, keepdims=True)
        vec_rows = dot(as_bf16(pick), vec[...])
        cent_rows = dot(as_bf16(member), cent[...].reshape(rows, width))
        residual = (vec_rows - cent_rows).astype(BF16)
        rot_load.wait()
        turned = dot(residual, rot[...])
        owner_wide = jnp.broadcast_to(owner_col, (per_shard, 128))
        turned = jnp.concatenate([turned, owner_wide], axis=1).T.astype(BF16)
        for c in range(NY):
            rows_out[c, 0:span] = turned[span * c : span * (c + 1)]
            rows_out[c, span : span + 16] = turned[width : width + 16]
    row_copies = [
        remote(rows_out.at[lax.rem(py + j, NY)], rows_in.at[j - 1],
               1, 1, {"cent": lax.rem(py + j, NY)})
        for j in range(1, NY)
    ]
    for copy in row_copies:
        copy.start()

    with scope("statwait"):
        wait_all(stat_in, recv_sem.at[0])
    levels = [stat_out[...]] + [stat_in[j] for j in range(NY - 1)]
    peak = levels[0]
    for item in levels[1:]:
        peak = jnp.maximum(peak, item)
    whole_total = jnp.exp(levels[0] - peak)
    for item in levels[1:]:
        whole_total += jnp.exp(item - peak)
    peak, whole_total = as_row(peak), as_row(whole_total)

    sibling = {"dp_2": lax.rem(pc + 1, NC)}
    x_side = [{"dp_0": lax.rem(px + j, NX)} for j in (1, NX - 1)]

    def core_copy(rx):
        at = pl.ds(128 * rx, 128)
        return remote(snd.at[at], rcv.at[at], 10 + rx, 2 + rx, sibling)

    moment_copy = remote(snd_m, rcv_m, 3, 6, sibling)

    def x_copy(q, j):
        return remote(xs[q].at[j], xr[q].at[j], 4 + q, 7 + 2 * q + (j > 1), x_side[j % 2])

    def z_copy(q, j):
        return remote(zs[q].at[j - 1], zr[q].at[j - 1], 6 + q, 11 + q,
                      {"dp_1": lax.rem(pz + j, NZ)})

    def last_copy(j):
        return remote(last.at[j], last_in.at[j - 1], 9, 14, {"dp_0": lax.rem(px + j, NX)})

    def sums(rx):
        at, sent = slice(128 * rx, 128 * (rx + 1)), slice(512 + 128 * rx, 640 + 128 * rx)
        factor = jnp.exp(tops[rx] - peak) / whole_total
        for side in (sent, at):
            got = score[side, :] * factor
            prob[side, :] = got.astype(BF16)
            parts = [got[:, 128 * j : 128 * (j + 1)] for j in range(8)]
            while len(parts) > 1:
                parts = [a + b for a, b in zip(parts[::2], parts[1::2])]
            weight[side, :] = parts[0]
        got = dot(jnp.concatenate([prob[sent, :], prob[at, :]], axis=0), vec[...])
        snd[at, :] = got[:128].astype(BF16)
        core_copy(rx).start()
        own[at, :] = got[128:]

    def split_mass(a):
        lane = iota(a.shape, 1)
        mass = jnp.where((lane >= span) & (lane < span + 2), a, 0.0)
        mass = jnp.sum(mass, axis=1, keepdims=True)
        high = mass.astype(BF16).astype(F32)
        return jnp.where(lane == span, high, jnp.where(lane == span + 1, mass - high, a))

    def moments():
        wait_all(rows_in, recv_sem.at[1])
        got = jnp.concatenate([rows_out[py]] + [rows_in[j] for j in range(NY - 1)], axis=1)
        turned_rows[...] = got[0:span].astype(F32)
        holders = got[span : span + 1].astype(F32)
        q = iota((64, 1), 0)
        qc, qx, qz = q // 32, (q // 8) % 4, q % 8
        wanted = (((px + qx) % NX) * NZ + (pz + qz) % NZ) * NC + (pc + qc) % NC
        chosen = as_bf16(wanted.astype(F32) == holders)
        filler = jnp.zeros((128 - span, rows), BF16)
        by_owner = moment.reshape(64, OWN, 128)
        for pair in range(SUB // 2):
            pieces = []
            for a in (2 * pair, 2 * pair + 1):
                for m in range(span // SUB):
                    block = turned_rows[SUB * m : SUB * (m + 1), :]
                    line = turned_rows[SUB * m + a : SUB * m + a + 1, :]
                    pieces.append((block * line).astype(BF16))
                pieces.append(filler)
            both = dot(chosen, jnp.concatenate(pieces, axis=0), ((1,), (1,)))
            for side in range(2):
                by_owner[:, 2 * pair + side, :] = both[:, 128 * side : 128 * (side + 1)]
        mass = jnp.sum(weight[...], axis=1, keepdims=True)
        both = split_mass(moment[...] + jnp.where(iota((rows, 128), 1) == span, mass, 0.0))
        snd_m[...] = both[512:].astype(BF16)
        moment_copy.start()
        own_m[...] = both[:512]

    def joined(rx):
        core_copy(rx).wait_recv()
        at = slice(128 * rx, 128 * (rx + 1))
        return own[at, :] + rcv[at, :].astype(F32)

    def columns(q):
        return slice(384 * q, 384 * (q + 1))

    def x_far():
        got = joined(2).astype(BF16)
        for q in range(2):
            for side in range(2):
                xs[q][side] = got[64 * side : 64 * (side + 1), columns(q)]
                x_copy(q, side).start()

    def x_plain(side):
        got = joined((1, 3)[side])
        plain, rest = (got[64:], got[:64]) if side == 0 else (got[:64], got[64:])
        for q in range(2):
            xs[q][2 + side] = plain[:, columns(q)].astype(BF16)
            x_copy(q, 2 + side).start()
        own[128 * (1 + side) : 128 * (1 + side) + 64, :] = rest

    def near():
        own[0:128, :] = joined(0)

    def x_add(q):
        wait_all(xr[q].at[pl.ds(0, 2)], recv_sem.at[7 + 2 * q])
        for side in range(2):
            rest = own[128 * (1 + side) : 128 * (1 + side) + 64, columns(q)]
            xs[q][4 + side] = (rest + xr[q][side].astype(F32)).astype(BF16)
            x_copy(q, 4 + side).start()

    def z_send(q):
        wait_all(xr[q].at[pl.ds(2, 4)], recv_sem.at[8 + 2 * q])
        low = own[0:64, columns(q)] + xr[q][4].astype(F32) + xr[q][3].astype(F32)
        high = own[64:128, columns(q)] + xr[q][2].astype(F32) + xr[q][5].astype(F32)
        block = [part[16 * j : 16 * (j + 1)] for part in (low, high) for j in range(4)]
        for j in (4, 3, 5, 2, 6, 1, 7):
            zs[q][j - 1] = block[j].astype(BF16)
            z_copy(q, j).start()
        own[0:OWN, columns(q)] = block[0]

    def finish(q):
        wait_all(zr[q], recv_sem.at[11 + q])
        got = own[0:OWN, columns(q)]
        for j in range(NZ - 1):
            got = got + zr[q][j].astype(F32)
        return got

    def moments_z():
        moment_copy.wait_recv()
        got = split_mass(own_m[...] + rcv_m[...].astype(F32)).reshape(NX, NZ, OWN, 128)
        for j in (4, 3, 5, 2, 6, 1, 7):
            zs[2][j - 1] = got[:, j].astype(BF16)
            z_copy(2, j).start()
        last[...] = got[:, 0]

    def moments_x():
        got = last[...]
        wait_all(zr[2], recv_sem.at[13])
        for j in range(NZ - 1):
            got = got + zr[2][j].astype(F32)
        last[...] = got
        for j in (2, 1, 3):
            last_copy(j).start()

    def moments_end():
        got = last[0]
        wait_all(last_in, recv_sem.at[14])
        for j in range(NX - 1):
            got = got + last_in[j]
        return got

    def staged(stage, *at):
        with scope(stage.__name__ + "".join(map(str, at))):
            return stage(*at)

    staged(sums, 2)
    staged(sums, 1)
    staged(x_far)
    staged(sums, 3)
    staged(x_plain, 0)
    staged(sums, 0)
    staged(x_plain, 1)
    staged(near)
    staged(moments)
    staged(x_add, 0)
    staged(x_add, 1)
    staged(moments_z)
    staged(z_send, 0)
    staged(z_send, 1)
    staged(moments_x)
    parts = [staged(finish, 0), staged(finish, 1), staged(moments_end)]
    lane = iota((OWN, 128), 1)
    mass = jnp.sum(
        jnp.where((lane >= span) & (lane < span + 2), parts[2], 0.0), axis=1, keepdims=True
    )
    first = ((px * NZ + pz) * NC + pc) * OWN
    mine = iota((OWN, rows), 1) == iota((OWN, rows), 0) + first
    prior_col = jnp.sum(jnp.where(mine, as_row(prior[...]), 0.0), axis=1, keepdims=True)
    own_cent = cent[px, pz, pc].astype(F32)
    new_ref[...] = (prior_col * own_cent + jnp.concatenate(parts[:2], axis=1)) / (prior_col + mass)
    mom_ref[...] = parts[2][:, :span] / rows

    with scope("endwaits"):
        sent = (stat_in, rows_in, snd, snd_m, xs0, xs1, zs0, zs1, zs2, last_in)
        for k, ref in enumerate(sent):
            if k != 2:
                wait_all(ref, send_sem.at[k])
        for rx in range(NX):
            core_copy(rx).wait_send()


def body(vectors, centroids, prior_mass, assign, owner_of, rotation):
    rows, width = vectors.shape
    span = width // NY
    half = rows // 2
    any_spec = pl.BlockSpec(memory_space=pl.ANY)
    vmem_spec = pl.BlockSpec(memory_space=pltpu.VMEM)
    dma = pltpu.SemaphoreType.DMA
    scratch = [
        pltpu.VMEM((rows, width), BF16),
        pltpu.VMEM((NX, NZ, NC, OWN, width), BF16),
        pltpu.VMEM((width, width), BF16),
        pltpu.VMEM((8, 128), F32),
        pltpu.VMEM((8, 128), jnp.int32),
        pltpu.VMEM((8, 128), jnp.int32),
        pltpu.VMEM((rows, rows), F32),
        pltpu.VMEM((rows, rows), BF16),
        pltpu.VMEM((rows, 128), F32),
        pltpu.VMEM((rows, 128), F32),
        pltpu.VMEM((8, 128), F32),
        pltpu.VMEM((NY - 1, 8, 128), F32),
        pltpu.VMEM((NY, span + 16, 128), BF16),
        pltpu.VMEM((NY - 1, span + 16, 128), BF16),
        pltpu.VMEM((span, rows), F32),
    ]
    scratch += [pltpu.VMEM((half, w), kind) for kind in (F32, BF16, BF16) for w in (width, 128)]
    scratch += [pltpu.VMEM((6, 64, 384), BF16)] * 4
    turns = [pltpu.VMEM((NZ - 1, OWN, 384), BF16)] * 2
    turns += [pltpu.VMEM((NZ - 1, NX, OWN, 128), BF16)]
    scratch += turns * 2 + [pltpu.VMEM((NX, OWN, 128), F32), pltpu.VMEM((NX - 1, OWN, 128), F32)]
    scratch += [dma((9,)), dma((14,)), dma((15,))]
    updated, moments = pl.pallas_call(
        kernel,
        out_shape=(
            jax.ShapeDtypeStruct((OWN, width), F32),
            jax.ShapeDtypeStruct((OWN, span), F32),
        ),
        in_specs=[any_spec] * 6,
        out_specs=(vmem_spec, vmem_spec),
        scratch_shapes=scratch,
        compiler_params=pltpu.CompilerParams(
            collective_id=0, has_side_effects=True, vmem_limit_bytes=40000 * 1024
        ),
    )(*(pltpu.with_memory_space_constraint(a, pltpu.HBM) for a in (
        vectors,
        centroids.reshape(NX, NZ, NC, OWN, width),
        rotation,
        prior_mass.reshape(8, 128),
        assign.reshape(8, 128),
        owner_of.reshape(NY, 8, 128),
    )))
    return (updated[None], moments[None])


def solution(mesh):
    finer = Mesh(
        mesh.devices.reshape(NX, NZ, NC, mesh.shape["cent"]), ("dp_0", "dp_1", "dp_2", "cent")
    )
    in_specs = (P(DP, None), P("cent", None), P("cent"), P(DP), P(), P())
    out_specs = (P("cent", DP, None), P(DP, None, "cent"))
    return jax.shard_map(body, mesh=finer, in_specs=in_specs, out_specs=out_specs, check_vma=False)
```

```python
import contextlib
import math

import jax
import jax.numpy as jnp
from jax import lax
from jax.experimental import pallas as pl
from jax.experimental.pallas import tpu as pltpu
from jax.sharding import Mesh
from jax.sharding import PartitionSpec as P

F32 = jnp.float32
BF16 = jnp.bfloat16
DP = ("dp_0", "dp_1", "dp_2")
NX, NZ, NC, NY = 4, 8, 2, 8
OWN = 16
SUB = 16
scope = contextlib.nullcontext


def dot(a, b, dims=((1,), (0,))):
    return lax.dot_general(a, b, (dims, ((), ())), preferred_element_type=F32)


def as_row(a):
    return jnp.concatenate([a[j : j + 1, :] for j in range(a.shape[0])], axis=1)


def as_bf16(mask):
    return mask.astype(F32).astype(BF16)


def iota(shape, dim):
    return lax.broadcasted_iota(jnp.int32, shape, dim)


def kernel(
    vec_hbm, cent_hbm, rot_hbm, prior_hbm, assign_hbm, owner_hbm, new_ref, mom_ref,
    vec, cent, rot, prior, assign, owner, score, prob, weight, moment,
    stat_out, stat_in, rows_out, rows_in, turned_rows,
    own, own_m, snd, snd_m, rcv, rcv_m,
    xs0, xs1, xr0, xr1, zs0, zs1, zs2, zr0, zr1, zr2, last, last_in, kept,
    load_sem, send_sem, recv_sem,
):
    xs, xr, zs, zr = (xs0, xs1), (xr0, xr1), (zs0, zs1, zs2), (zr0, zr1, zr2)
    px, pz, pc = (lax.axis_index(name) for name in DP)
    py = lax.axis_index("cent")
    rows, width = vec.shape
    per_shard = rows // NY
    span = width // NY
    inv_root = 1.0 / math.sqrt(width)

    def load(k, src, dst):
        return pltpu.make_async_copy(src, dst, load_sem.at[k])

    def wait_all(ref, sem):
        pltpu.make_async_copy(ref, ref, sem).wait()

    cent_loads = [
        load(k, cent_hbm.at[lax.rem(px + k, NX)], cent.at[lax.rem(px + k, NX)])
        for k in range(NX)
    ]
    small_loads = [
        load(5, assign_hbm, assign), load(6, owner_hbm.at[py], owner), load(7, prior_hbm, prior)
    ]
    rot_load = load(8, rot_hbm, rot)
    for k in range(4):
        load(4, vec_hbm.at[pl.ds(256 * k, 256)], vec.at[pl.ds(256 * k, 256)]).start()
    cent_loads[0].start()

    barrier = pltpu.get_barrier_semaphore()
    partners = [{"cent": lax.rem(py + j, NY)} for j in range(1, NY)]
    partners += [{"dp_2": lax.rem(pc + 1, NC)}]
    partners += [{"dp_0": lax.rem(px + j, NX)} for j in range(1, NX)]
    partners += [{"dp_1": lax.rem(pz + j, NZ)} for j in range(1, NZ)]
    for partner in partners:
        pl.semaphore_signal(
            barrier, inc=1, device_id=partner, device_id_type=pl.DeviceIdType.MESH
        )

    for item in cent_loads[1:]:
        item.start()

    def remote(src, dst, ss, rs, device):
        return pltpu.make_async_remote_copy(
            src_ref=src, dst_ref=dst, send_sem=send_sem.at[ss], recv_sem=recv_sem.at[rs],
            device_id=device, device_id_type=pl.DeviceIdType.MESH,
        )

    with scope("loadwait"):
        wait_all(vec, load_sem.at[4])
    for item in small_loads + [rot_load]:
        item.start()
    tops, total = [], None
    with scope("score"):
        cent_loads[0].wait()
        for rx in range(NX + 1):
            if rx < NX:
                blocks = [
                    cent[lax.rem(px + rx, NX), lax.rem(pz + rz, NZ), lax.rem(pc + rc, NC)]
                    for rc in range(NC)
                    for rz in range(NZ)
                ]
                lhs = jnp.concatenate(blocks, axis=0)
                wide = lhs.astype(F32)
                square = jnp.sum(wide * wide, axis=1, keepdims=True)
                got = (2.0 * dot(lhs, vec[...], ((1,), (1,))) - square) * inv_root
                for rc in range(NC):
                    at = 512 * rc + 128 * rx
                    score[at : at + 128, :] = got[128 * rc : 128 * (rc + 1)]
                top = jnp.max(jnp.max(got.reshape(32, 8, rows), axis=0), axis=0, keepdims=True)
                tops.append(jnp.maximum(top, tops[-1]) if rx else top)
            if rx == 0:
                for item in cent_loads[1:]:
                    item.wait()
            else:
                top, part = tops[rx - 1], jnp.zeros((8, rows), F32)
                for rc in range(NC):
                    at = 512 * rc + 128 * (rx - 1)
                    got = jnp.exp(score[at : at + 128, :] - top)
                    score[at : at + 128, :] = got
                    part = part + jnp.sum(got.reshape(16, 8, rows), axis=0)
                total = part + total * jnp.exp(tops[rx - 2] - top) if rx > 1 else part
    level = tops[-1] + jnp.log(jnp.sum(total, axis=0, keepdims=True))
    for j in range(8):
        stat_out[j : j + 1, :] = level[:, 128 * j : 128 * (j + 1)]

    with scope("barrier"):
        pl.semaphore_wait(barrier, len(partners))
    stat_copies = [
        remote(stat_out, stat_in.at[j - 1], 0, 0,
               {"cent": lax.rem(py + j, NY)})
        for j in range(1, NY)
    ]
    for copy in stat_copies:
        copy.start()

    with scope("rows"):
        for item in small_loads:
            item.wait()
        lists = assign[...]
        inside = lax.shift_right_logical(lists, 10) == py
        flag = as_bf16(inside)
        before = dot(flag, as_bf16(iota((128, 128), 0) < iota((128, 128), 1)))
        whole = dot(flag, jnp.ones((128, 128), BF16)).astype(BF16)
        earlier = dot(as_bf16(iota((8, 8), 1) < iota((8, 8), 0)), whole)
        rank = jnp.where(inside, before + earlier, -1.0)
        local = jnp.bitwise_and(lists, 1023).astype(F32)
        pick = iota((per_shard, rows), 0).astype(F32) == as_row(rank)
        list_of = jnp.sum(jnp.where(pick, as_row(local), 0.0), axis=1, keepdims=True)
        member = iota((per_shard, rows), 1).astype(F32) == list_of
        holder = as_row(owner[...].astype(F32))
        owner_col = jnp.sum(jnp.where(member, holder, 0.0), axis=1, keepdims=True)
        vec_rows = dot(as_bf16(pick), vec[...])
        cent_rows = dot(as_bf16(member), cent[...].reshape(rows, width))
        residual = (vec_rows - cent_rows).astype(BF16)
        rot_load.wait()
        turned = dot(residual, rot[...])
        owner_wide = jnp.broadcast_to(owner_col, (per_shard, 128))
        turned = jnp.concatenate([turned, owner_wide], axis=1).T.astype(BF16)
        for c in range(NY):
            rows_out[c, 0:span] = turned[span * c : span * (c + 1)]
            rows_out[c, span : span + 16] = turned[width : width + 16]
    row_copies = [
        remote(rows_out.at[lax.rem(py + j, NY)], rows_in.at[j - 1],
               1, 1, {"cent": lax.rem(py + j, NY)})
        for j in range(1, NY)
    ]
    for copy in row_copies:
        copy.start()

    with scope("statwait"):
        wait_all(stat_in, recv_sem.at[0])
    levels = [stat_out[...]] + [stat_in[j] for j in range(NY - 1)]
    peak = levels[0]
    for item in levels[1:]:
        peak = jnp.maximum(peak, item)
    whole_total = jnp.exp(levels[0] - peak)
    for item in levels[1:]:
        whole_total += jnp.exp(item - peak)
    peak, whole_total = as_row(peak), as_row(whole_total)

    sibling = {"dp_2": lax.rem(pc + 1, NC)}
    x_side = [{"dp_0": lax.rem(px + j, NX)} for j in (1, NX - 1)]

    def core_copy(rx):
        at = pl.ds(128 * rx, 128)
        return remote(snd.at[at], rcv.at[at], 10 + rx, 2 + rx, sibling)

    moment_copy = remote(snd_m, rcv_m, 3, 6, sibling)

    def x_copy(q, j):
        return remote(xs[q].at[j], xr[q].at[j], 4 + q, 7 + 2 * q + (j > 1), x_side[j % 2])

    def z_copy(q, j):
        relayed = q != 1 and j == 4
        return remote(zs[q].at[j - 1], zr[q].at[j - 1], 6 + q, 15 + q // 2 if relayed else 11 + q,
                      {"dp_1": lax.rem(pz + (6 if relayed else j), NZ)})

    def last_copy(j):
        return remote(last.at[j], last_in.at[j - 1], 9, 14, {"dp_0": lax.rem(px + j, NX)})

    def sums(rx):
        at, sent = slice(128 * rx, 128 * (rx + 1)), slice(512 + 128 * rx, 640 + 128 * rx)
        factor = jnp.exp(tops[rx] - peak) / whole_total
        for side in (sent, at):
            got = score[side, :] * factor
            prob[side, :] = got.astype(BF16)
            parts = [got[:, 128 * j : 128 * (j + 1)] for j in range(8)]
            while len(parts) > 1:
                parts = [a + b for a, b in zip(parts[::2], parts[1::2])]
            weight[side, :] = parts[0]
        got = dot(jnp.concatenate([prob[sent, :], prob[at, :]], axis=0), vec[...])
        snd[at, :] = got[:128].astype(BF16)
        core_copy(rx).start()
        own[at, :] = got[128:]

    def split_mass(a):
        lane = iota(a.shape, 1)
        mass = jnp.where((lane >= span) & (lane < span + 2), a, 0.0)
        mass = jnp.sum(mass, axis=1, keepdims=True)
        high = mass.astype(BF16).astype(F32)
        return jnp.where(lane == span, high, jnp.where(lane == span + 1, mass - high, a))

    def owners():
        wait_all(rows_in, recv_sem.at[1])
        got = jnp.concatenate([rows_out[py]] + [rows_in[j] for j in range(NY - 1)], axis=1)
        turned_rows[...] = got[0:span].astype(F32)
        holders = got[span : span + 1].astype(F32)
        q = iota((64, 1), 0)
        qc, qx, qz = q // 32, (q // 8) % 4, q % 8
        wanted = (((px + qx) % NX) * NZ + (pz + qz) % NZ) * NC + (pc + qc) % NC
        return as_bf16(wanted.astype(F32) == holders)

    def moments(chosen, pairs):
        filler = jnp.zeros((128 - span, rows), BF16)
        by_owner = moment.reshape(64, OWN, 128)
        for pair in pairs:
            pieces = []
            for a in (2 * pair, 2 * pair + 1):
                for m in range(span // SUB):
                    block = turned_rows[SUB * m : SUB * (m + 1), :]
                    line = turned_rows[SUB * m + a : SUB * m + a + 1, :]
                    pieces.append((block * line).astype(BF16))
                pieces.append(filler)
            both = dot(chosen, jnp.concatenate(pieces, axis=0), ((1,), (1,)))
            for side in range(2):
                by_owner[:, 2 * pair + side, :] = both[:, 128 * side : 128 * (side + 1)]

    def moments_core():
        mass = jnp.sum(weight[...], axis=1, keepdims=True)
        both = split_mass(moment[...] + jnp.where(iota((rows, 128), 1) == span, mass, 0.0))
        snd_m[...] = both[512:].astype(BF16)
        moment_copy.start()
        own_m[...] = both[:512]

    def joined(rx):
        core_copy(rx).wait_recv()
        at = slice(128 * rx, 128 * (rx + 1))
        return own[at, :] + rcv[at, :].astype(F32)

    def columns(q):
        return slice(384 * q, 384 * (q + 1))

    def x_far():
        got = joined(2).astype(BF16)
        for q in range(2):
            for side in range(2):
                xs[q][side] = got[64 * side : 64 * (side + 1), columns(q)]
                x_copy(q, side).start()

    def x_plain(side):
        got = joined((1, 3)[side])
        plain, rest = (got[64:], got[:64]) if side == 0 else (got[:64], got[64:])
        for q in range(2):
            xs[q][2 + side] = plain[:, columns(q)].astype(BF16)
            x_copy(q, 2 + side).start()
        own[128 * (1 + side) : 128 * (1 + side) + 64, :] = rest

    def near():
        own[0:128, :] = joined(0)

    def x_add(q):
        wait_all(xr[q].at[pl.ds(0, 2)], recv_sem.at[7 + 2 * q])
        for side in range(2):
            rest = own[128 * (1 + side) : 128 * (1 + side) + 64, columns(q)]
            xs[q][4 + side] = (rest + xr[q][side].astype(F32)).astype(BF16)
            x_copy(q, 4 + side).start()

    def z_send(q):
        wait_all(xr[q].at[pl.ds(2, 4)], recv_sem.at[8 + 2 * q])
        low = own[0:64, columns(q)] + xr[q][4].astype(F32) + xr[q][3].astype(F32)
        high = own[64:128, columns(q)] + xr[q][2].astype(F32) + xr[q][5].astype(F32)
        block = [part[16 * j : 16 * (j + 1)] for part in (low, high) for j in range(4)]
        for j in (4, 3, 5, 2, 6, 1, 7):
            if q == 0 and j == 6:
                own[96:112, columns(q)] = block[j]
                continue
            zs[q][j - 1] = block[j].astype(BF16)
            z_copy(q, j).start()
        own[0:OWN, columns(q)] = block[0]

    def z_relay():
        wait_all(zr[0].at[pl.ds(3, 1)], recv_sem.at[15])
        zs[0][5] = (own[96:112, columns(0)] + zr[0][3].astype(F32)).astype(BF16)
        z_copy(0, 6).start()

    def finish(q):
        wait_all(zr[q] if q else zr[q].at[pl.ds(0, 6)], recv_sem.at[11 + q])
        got = own[0:OWN, columns(q)]
        for j in range(NZ - 1):
            if q or j != 3:
                got = got + zr[q][j].astype(F32)
        return got

    def moments_z():
        moment_copy.wait_recv()
        got = split_mass(own_m[...] + rcv_m[...].astype(F32)).reshape(NX, NZ, OWN, 128)
        for j in (4, 3, 5, 2, 1, 7):
            zs[2][j - 1] = got[:, j].astype(BF16)
            z_copy(2, j).start()
        last[...] = got[:, 0]
        kept[...] = got[:, 6]

    def moments_relay():
        wait_all(zr[2].at[pl.ds(3, 1)], recv_sem.at[16])
        got = (kept[...] + zr[2][3].astype(F32)).reshape(NX * OWN, 128)
        zs[2][5] = split_mass(got).reshape(NX, OWN, 128).astype(BF16)
        z_copy(2, 6).start()

    def moments_x():
        got = last[...]
        wait_all(zr[2].at[pl.ds(0, 6)], recv_sem.at[13])
        for j in (0, 1, 2, 4, 5, 6):
            got = got + zr[2][j].astype(F32)
        last[...] = got
        for j in (2, 1, 3):
            last_copy(j).start()

    def moments_end():
        got = last[0]
        wait_all(last_in, recv_sem.at[14])
        for j in range(NX - 1):
            got = got + last_in[j]
        return got

    def staged(stage, *at):
        with scope(stage.__name__ + "".join(map(str, at))):
            return stage(*at)

    staged(sums, 2)
    staged(sums, 1)
    staged(x_far)
    staged(sums, 3)
    staged(x_plain, 0)
    staged(sums, 0)
    with scope("moments_1"):
        chosen = owners()
        moments(chosen, range(0, 4))
    staged(x_plain, 1)
    with scope("moments_2"):
        moments(chosen, range(4, 8))
        moments_core()
    staged(x_add, 0)
    staged(x_add, 1)
    staged(near)
    staged(moments_z)
    staged(z_send, 0)
    staged(moments_relay)
    staged(z_send, 1)
    staged(z_relay)
    staged(moments_x)
    parts = [staged(finish, 0), staged(finish, 1), staged(moments_end)]
    lane = iota((OWN, 128), 1)
    mass = jnp.sum(
        jnp.where((lane >= span) & (lane < span + 2), parts[2], 0.0), axis=1, keepdims=True
    )
    first = ((px * NZ + pz) * NC + pc) * OWN
    mine = iota((OWN, rows), 1) == iota((OWN, rows), 0) + first
    prior_col = jnp.sum(jnp.where(mine, as_row(prior[...]), 0.0), axis=1, keepdims=True)
    own_cent = cent[px, pz, pc].astype(F32)
    new_ref[...] = (prior_col * own_cent + jnp.concatenate(parts[:2], axis=1)) / (prior_col + mass)
    mom_ref[...] = parts[2][:, :span] / rows

    with scope("endwaits"):
        sent = (stat_in, rows_in, snd, snd_m, xs0, xs1, zs0, zs1, zs2, last_in)
        for k, ref in enumerate(sent):
            if k != 2:
                wait_all(ref, send_sem.at[k])
        for rx in range(NX):
            core_copy(rx).wait_send()


def body(vectors, centroids, prior_mass, assign, owner_of, rotation):
    rows, width = vectors.shape
    span = width // NY
    half = rows // 2
    any_spec = pl.BlockSpec(memory_space=pl.ANY)
    vmem_spec = pl.BlockSpec(memory_space=pltpu.VMEM)
    dma = pltpu.SemaphoreType.DMA
    scratch = [
        pltpu.VMEM((rows, width), BF16),
        pltpu.VMEM((NX, NZ, NC, OWN, width), BF16),
        pltpu.VMEM((width, width), BF16),
        pltpu.VMEM((8, 128), F32),
        pltpu.VMEM((8, 128), jnp.int32),
        pltpu.VMEM((8, 128), jnp.int32),
        pltpu.VMEM((rows, rows), F32),
        pltpu.VMEM((rows, rows), BF16),
        pltpu.VMEM((rows, 128), F32),
        pltpu.VMEM((rows, 128), F32),
        pltpu.VMEM((8, 128), F32),
        pltpu.VMEM((NY - 1, 8, 128), F32),
        pltpu.VMEM((NY, span + 16, 128), BF16),
        pltpu.VMEM((NY - 1, span + 16, 128), BF16),
        pltpu.VMEM((span, rows), F32),
    ]
    scratch += [pltpu.VMEM((half, w), kind) for kind in (F32, BF16, BF16) for w in (width, 128)]
    scratch += [pltpu.VMEM((6, 64, 384), BF16)] * 4
    turns = [pltpu.VMEM((NZ - 1, OWN, 384), BF16)] * 2
    turns += [pltpu.VMEM((NZ - 1, NX, OWN, 128), BF16)]
    scratch += turns * 2 + [pltpu.VMEM((NX, OWN, 128), F32), pltpu.VMEM((NX - 1, OWN, 128), F32)]
    scratch += [pltpu.VMEM((NX, OWN, 128), F32)]
    scratch += [dma((9,)), dma((14,)), dma((17,))]
    updated, moments = pl.pallas_call(
        kernel,
        out_shape=(
            jax.ShapeDtypeStruct((OWN, width), F32),
            jax.ShapeDtypeStruct((OWN, span), F32),
        ),
        in_specs=[any_spec] * 6,
        out_specs=(vmem_spec, vmem_spec),
        scratch_shapes=scratch,
        compiler_params=pltpu.CompilerParams(
            collective_id=0, has_side_effects=True, vmem_limit_bytes=40000 * 1024
        ),
    )(*(pltpu.with_memory_space_constraint(a, pltpu.HBM) for a in (
        vectors,
        centroids.reshape(NX, NZ, NC, OWN, width),
        rotation,
        prior_mass.reshape(8, 128),
        assign.reshape(8, 128),
        owner_of.reshape(NY, 8, 128),
    )))
    return (updated[None], moments[None])


def solution(mesh):
    finer = Mesh(
        mesh.devices.reshape(NX, NZ, NC, mesh.shape["cent"]), ("dp_0", "dp_1", "dp_2", "cent")
    )
    in_specs = (P(DP, None), P("cent", None), P("cent"), P(DP), P(), P())
    out_specs = (P("cent", DP, None), P(DP, None, "cent"))
    return jax.shard_map(body, mesh=finer, in_specs=in_specs, out_specs=out_specs, check_vma=False)
```

```python
import contextlib
import math

import jax
import jax.numpy as jnp
from jax import lax
from jax.experimental import pallas as pl
from jax.experimental.pallas import tpu as pltpu
from jax.sharding import Mesh
from jax.sharding import PartitionSpec as P

F32 = jnp.float32
BF16 = jnp.bfloat16
DP = ("dp_0", "dp_1", "dp_2")
NX, NZ, NC, NY = 4, 8, 2, 8
OWN = 16
EDGES = (0, 256, 768)
SUB = 16
scope = contextlib.nullcontext


def dot(a, b, dims=((1,), (0,))):
    return lax.dot_general(a, b, (dims, ((), ())), preferred_element_type=F32)


def as_row(a):
    return jnp.concatenate([a[j : j + 1, :] for j in range(a.shape[0])], axis=1)


def as_bf16(mask):
    return mask.astype(F32).astype(BF16)


def iota(shape, dim):
    return lax.broadcasted_iota(jnp.int32, shape, dim)


def kernel(
    vec_hbm, cent_hbm, rot_hbm, prior_hbm, assign_hbm, owner_hbm, new_ref, mom_ref,
    vec, cent, rot, prior, assign, owner, score, prob, weight, moment,
    stat_out, stat_in, rows_out, rows_in, turned_rows,
    own, own_m, snd, snd_m, rcv, rcv_m,
    xs0, xs1, xr0, xr1, zs0, zs1, zs2, zr0, zr1, zr2, last, last_in, kept,
    load_sem, send_sem, recv_sem,
):
    xs, xr, zs, zr = (xs0, xs1), (xr0, xr1), (zs0, zs1, zs2), (zr0, zr1, zr2)
    px, pz, pc = (lax.axis_index(name) for name in DP)
    py = lax.axis_index("cent")
    rows, width = vec.shape
    per_shard = rows // NY
    span = width // NY
    inv_root = 1.0 / math.sqrt(width)

    def load(k, src, dst):
        return pltpu.make_async_copy(src, dst, load_sem.at[k])

    def wait_all(ref, sem):
        pltpu.make_async_copy(ref, ref, sem).wait()

    cent_loads = [
        load(k, cent_hbm.at[lax.rem(px + k, NX)], cent.at[lax.rem(px + k, NX)])
        for k in range(NX)
    ]
    small_loads = [
        load(5, assign_hbm, assign), load(6, owner_hbm.at[py], owner), load(7, prior_hbm, prior)
    ]
    rot_load = load(8, rot_hbm, rot)
    for k in range(4):
        load(4, vec_hbm.at[pl.ds(256 * k, 256)], vec.at[pl.ds(256 * k, 256)]).start()
    cent_loads[0].start()

    barrier = pltpu.get_barrier_semaphore()
    partners = [{"cent": lax.rem(py + j, NY)} for j in range(1, NY)]
    partners += [{"dp_2": lax.rem(pc + 1, NC)}]
    partners += [{"dp_0": lax.rem(px + j, NX)} for j in range(1, NX)]
    partners += [{"dp_1": lax.rem(pz + j, NZ)} for j in range(1, NZ)]
    for partner in partners:
        pl.semaphore_signal(
            barrier, inc=1, device_id=partner, device_id_type=pl.DeviceIdType.MESH
        )

    for item in cent_loads[1:]:
        item.start()

    def remote(src, dst, ss, rs, device):
        return pltpu.make_async_remote_copy(
            src_ref=src, dst_ref=dst, send_sem=send_sem.at[ss], recv_sem=recv_sem.at[rs],
            device_id=device, device_id_type=pl.DeviceIdType.MESH,
        )

    with scope("loadwait"):
        wait_all(vec, load_sem.at[4])
    for item in small_loads + [rot_load]:
        item.start()
    tops, total = [], None
    with scope("score"):
        cent_loads[0].wait()
        for rx in range(NX + 1):
            if rx < NX:
                blocks = [
                    cent[lax.rem(px + rx, NX), lax.rem(pz + rz, NZ), lax.rem(pc + rc, NC)]
                    for rc in range(NC)
                    for rz in range(NZ)
                ]
                lhs = jnp.concatenate(blocks, axis=0)
                wide = lhs.astype(F32)
                square = jnp.sum(wide * wide, axis=1, keepdims=True)
                got = (2.0 * dot(lhs, vec[...], ((1,), (1,))) - square) * inv_root
                for rc in range(NC):
                    at = 512 * rc + 128 * rx
                    score[at : at + 128, :] = got[128 * rc : 128 * (rc + 1)]
                top = jnp.max(jnp.max(got.reshape(32, 8, rows), axis=0), axis=0, keepdims=True)
                tops.append(jnp.maximum(top, tops[-1]) if rx else top)
            if rx == 0:
                for item in cent_loads[1:]:
                    item.wait()
            else:
                top, part = tops[rx - 1], jnp.zeros((8, rows), F32)
                for rc in range(NC):
                    at = 512 * rc + 128 * (rx - 1)
                    got = jnp.exp(score[at : at + 128, :] - top)
                    score[at : at + 128, :] = got
                    part = part + jnp.sum(got.reshape(16, 8, rows), axis=0)
                total = part + total * jnp.exp(tops[rx - 2] - top) if rx > 1 else part
    level = tops[-1] + jnp.log(jnp.sum(total, axis=0, keepdims=True))
    for j in range(8):
        stat_out[j : j + 1, :] = level[:, 128 * j : 128 * (j + 1)]

    with scope("barrier"):
        pl.semaphore_wait(barrier, len(partners))
    stat_copies = [
        remote(stat_out, stat_in.at[j - 1], 0, 0,
               {"cent": lax.rem(py + j, NY)})
        for j in range(1, NY)
    ]
    for copy in stat_copies:
        copy.start()

    with scope("rows"):
        for item in small_loads:
            item.wait()
        lists = assign[...]
        inside = lax.shift_right_logical(lists, 10) == py
        flag = as_bf16(inside)
        before = dot(flag, as_bf16(iota((128, 128), 0) < iota((128, 128), 1)))
        whole = dot(flag, jnp.ones((128, 128), BF16)).astype(BF16)
        earlier = dot(as_bf16(iota((8, 8), 1) < iota((8, 8), 0)), whole)
        rank = jnp.where(inside, before + earlier, -1.0)
        local = jnp.bitwise_and(lists, 1023).astype(F32)
        pick = iota((per_shard, rows), 0).astype(F32) == as_row(rank)
        list_of = jnp.sum(jnp.where(pick, as_row(local), 0.0), axis=1, keepdims=True)
        member = iota((per_shard, rows), 1).astype(F32) == list_of
        holder = as_row(owner[...].astype(F32))
        owner_col = jnp.sum(jnp.where(member, holder, 0.0), axis=1, keepdims=True)
        vec_rows = dot(as_bf16(pick), vec[...])
        cent_rows = dot(as_bf16(member), cent[...].reshape(rows, width))
        residual = (vec_rows - cent_rows).astype(BF16)
        rot_load.wait()
        turned = dot(residual, rot[...])
        owner_wide = jnp.broadcast_to(owner_col, (per_shard, 128))
        turned = jnp.concatenate([turned, owner_wide], axis=1).T.astype(BF16)
        for c in range(NY):
            rows_out[c, 0:span] = turned[span * c : span * (c + 1)]
            rows_out[c, span : span + 16] = turned[width : width + 16]
    row_copies = [
        remote(rows_out.at[lax.rem(py + j, NY)], rows_in.at[j - 1],
               1, 1, {"cent": lax.rem(py + j, NY)})
        for j in range(1, NY)
    ]
    for copy in row_copies:
        copy.start()

    with scope("statwait"):
        wait_all(stat_in, recv_sem.at[0])
    levels = [stat_out[...]] + [stat_in[j] for j in range(NY - 1)]
    peak = levels[0]
    for item in levels[1:]:
        peak = jnp.maximum(peak, item)
    whole_total = jnp.exp(levels[0] - peak)
    for item in levels[1:]:
        whole_total += jnp.exp(item - peak)
    peak, whole_total = as_row(peak), as_row(whole_total)

    sibling = {"dp_2": lax.rem(pc + 1, NC)}
    x_side = [{"dp_0": lax.rem(px + j, NX)} for j in (1, NX - 1)]

    def core_copy(rx):
        at = pl.ds(128 * rx, 128)
        return remote(snd.at[at], rcv.at[at], 10 + rx, 2 + rx, sibling)

    moment_copy = remote(snd_m, rcv_m, 3, 6, sibling)

    def x_copy(q, j):
        return remote(xs[q].at[j], xr[q].at[j], 4 + q, 7 + 2 * q + (j > 1), x_side[j % 2])

    def z_copy(q, j):
        relayed = q != 1 and j == 4
        return remote(zs[q].at[j - 1], zr[q].at[j - 1], 6 + q, 15 + q // 2 if relayed else 11 + q,
                      {"dp_1": lax.rem(pz + (6 if relayed else j), NZ)})

    def last_copy(j):
        return remote(last.at[j], last_in.at[j - 1], 9, 14, {"dp_0": lax.rem(px + j, NX)})

    def sums(rx):
        at, sent = slice(128 * rx, 128 * (rx + 1)), slice(512 + 128 * rx, 640 + 128 * rx)
        factor = jnp.exp(tops[rx] - peak) / whole_total
        for side in (sent, at):
            got = score[side, :] * factor
            prob[side, :] = got.astype(BF16)
            parts = [got[:, 128 * j : 128 * (j + 1)] for j in range(8)]
            while len(parts) > 1:
                parts = [a + b for a, b in zip(parts[::2], parts[1::2])]
            weight[side, :] = parts[0]
        got = dot(jnp.concatenate([prob[sent, :], prob[at, :]], axis=0), vec[...])
        snd[at, :] = got[:128].astype(BF16)
        core_copy(rx).start()
        own[at, :] = got[128:]

    def split_mass(a):
        lane = iota(a.shape, 1)
        mass = jnp.where((lane >= span) & (lane < span + 2), a, 0.0)
        mass = jnp.sum(mass, axis=1, keepdims=True)
        high = mass.astype(BF16).astype(F32)
        return jnp.where(lane == span, high, jnp.where(lane == span + 1, mass - high, a))

    def owners():
        wait_all(rows_in, recv_sem.at[1])
        got = jnp.concatenate([rows_out[py]] + [rows_in[j] for j in range(NY - 1)], axis=1)
        turned_rows[...] = got[0:span].astype(F32)
        holders = got[span : span + 1].astype(F32)
        q = iota((64, 1), 0)
        qc, qx, qz = q // 32, (q // 8) % 4, q % 8
        wanted = (((px + qx) % NX) * NZ + (pz + qz) % NZ) * NC + (pc + qc) % NC
        return as_bf16(wanted.astype(F32) == holders)

    def moments(chosen, pairs):
        filler = jnp.zeros((128 - span, rows), BF16)
        by_owner = moment.reshape(64, OWN, 128)
        for pair in pairs:
            pieces = []
            for a in (2 * pair, 2 * pair + 1):
                for m in range(span // SUB):
                    block = turned_rows[SUB * m : SUB * (m + 1), :]
                    line = turned_rows[SUB * m + a : SUB * m + a + 1, :]
                    pieces.append((block * line).astype(BF16))
                pieces.append(filler)
            both = dot(chosen, jnp.concatenate(pieces, axis=0), ((1,), (1,)))
            for side in range(2):
                by_owner[:, 2 * pair + side, :] = both[:, 128 * side : 128 * (side + 1)]

    def moments_core():
        mass = jnp.sum(weight[...], axis=1, keepdims=True)
        both = split_mass(moment[...] + jnp.where(iota((rows, 128), 1) == span, mass, 0.0))
        snd_m[...] = both[512:].astype(BF16)
        moment_copy.start()
        own_m[...] = both[:512]

    def joined(rx):
        core_copy(rx).wait_recv()
        at = slice(128 * rx, 128 * (rx + 1))
        return own[at, :] + rcv[at, :].astype(F32)

    def columns(q):
        return slice(EDGES[q], EDGES[q + 1])

    def x_far():
        got = joined(2).astype(BF16)
        for q in range(2):
            for side in range(2):
                xs[q][side] = got[64 * side : 64 * (side + 1), columns(q)]
                x_copy(q, side).start()

    def x_plain(side):
        got = joined((1, 3)[side])
        plain, rest = (got[64:], got[:64]) if side == 0 else (got[:64], got[64:])
        for q in range(2):
            xs[q][2 + side] = plain[:, columns(q)].astype(BF16)
            x_copy(q, 2 + side).start()
        own[128 * (1 + side) : 128 * (1 + side) + 64, :] = rest

    def near():
        own[0:128, :] = joined(0)

    def x_add(q):
        wait_all(xr[q].at[pl.ds(0, 2)], recv_sem.at[7 + 2 * q])
        for side in range(2):
            rest = own[128 * (1 + side) : 128 * (1 + side) + 64, columns(q)]
            xs[q][4 + side] = (rest + xr[q][side].astype(F32)).astype(BF16)
            x_copy(q, 4 + side).start()

    def z_send(q):
        wait_all(xr[q].at[pl.ds(2, 4)], recv_sem.at[8 + 2 * q])
        low = own[0:64, columns(q)] + xr[q][4].astype(F32) + xr[q][3].astype(F32)
        high = own[64:128, columns(q)] + xr[q][2].astype(F32) + xr[q][5].astype(F32)
        block = [part[16 * j : 16 * (j + 1)] for part in (low, high) for j in range(4)]
        for j in (4, 3, 5, 2, 6, 1, 7):
            if q == 0 and j == 6:
                own[96:112, columns(q)] = block[j]
                continue
            zs[q][j - 1] = block[j].astype(BF16)
            z_copy(q, j).start()
        own[0:OWN, columns(q)] = block[0]

    def z_relay():
        wait_all(zr[0].at[pl.ds(3, 1)], recv_sem.at[15])
        zs[0][5] = (own[96:112, columns(0)] + zr[0][3].astype(F32)).astype(BF16)
        z_copy(0, 6).start()

    def finish(q):
        wait_all(zr[q] if q else zr[q].at[pl.ds(0, 6)], recv_sem.at[11 + q])
        got = own[0:OWN, columns(q)]
        for j in range(NZ - 1):
            if q or j != 3:
                got = got + zr[q][j].astype(F32)
        return got

    def moments_z():
        moment_copy.wait_recv()
        got = split_mass(own_m[...] + rcv_m[...].astype(F32)).reshape(NX, NZ, OWN, 128)
        for j in (4, 3, 5, 2, 1, 7):
            zs[2][j - 1] = got[:, j].astype(BF16)
            z_copy(2, j).start()
        last[...] = got[:, 0]
        kept[...] = got[:, 6]

    def moments_relay():
        wait_all(zr[2].at[pl.ds(3, 1)], recv_sem.at[16])
        got = (kept[...] + zr[2][3].astype(F32)).reshape(NX * OWN, 128)
        zs[2][5] = split_mass(got).reshape(NX, OWN, 128).astype(BF16)
        z_copy(2, 6).start()

    def moments_x():
        got = last[...]
        wait_all(zr[2].at[pl.ds(0, 6)], recv_sem.at[13])
        for j in (0, 1, 2, 4, 5, 6):
            got = got + zr[2][j].astype(F32)
        last[...] = got
        for j in (2, 1, 3):
            last_copy(j).start()

    def moments_end():
        got = last[0]
        wait_all(last_in, recv_sem.at[14])
        for j in range(NX - 1):
            got = got + last_in[j]
        return got

    def staged(stage, *at):
        with scope(stage.__name__ + "".join(map(str, at))):
            return stage(*at)

    staged(sums, 2)
    staged(sums, 1)
    staged(x_far)
    staged(sums, 3)
    staged(x_plain, 0)
    staged(sums, 0)
    with scope("moments_1"):
        chosen = owners()
        moments(chosen, range(0, 4))
    staged(x_plain, 1)
    with scope("moments_2"):
        moments(chosen, range(4, 8))
        moments_core()
    staged(x_add, 0)
    staged(x_add, 1)
    staged(near)
    staged(moments_z)
    staged(z_send, 0)
    staged(moments_relay)
    staged(z_send, 1)
    staged(z_relay)
    staged(moments_x)
    parts = [staged(finish, 0), staged(finish, 1), staged(moments_end)]
    lane = iota((OWN, 128), 1)
    mass = jnp.sum(
        jnp.where((lane >= span) & (lane < span + 2), parts[2], 0.0), axis=1, keepdims=True
    )
    first = ((px * NZ + pz) * NC + pc) * OWN
    mine = iota((OWN, rows), 1) == iota((OWN, rows), 0) + first
    prior_col = jnp.sum(jnp.where(mine, as_row(prior[...]), 0.0), axis=1, keepdims=True)
    own_cent = cent[px, pz, pc].astype(F32)
    new_ref[...] = (prior_col * own_cent + jnp.concatenate(parts[:2], axis=1)) / (prior_col + mass)
    mom_ref[...] = parts[2][:, :span] / rows

    with scope("endwaits"):
        sent = (stat_in, rows_in, snd, snd_m, xs0, xs1, zs0, zs1, zs2, last_in)
        for k, ref in enumerate(sent):
            if k != 2:
                wait_all(ref, send_sem.at[k])
        for rx in range(NX):
            core_copy(rx).wait_send()


def body(vectors, centroids, prior_mass, assign, owner_of, rotation):
    rows, width = vectors.shape
    span = width // NY
    half = rows // 2
    any_spec = pl.BlockSpec(memory_space=pl.ANY)
    vmem_spec = pl.BlockSpec(memory_space=pltpu.VMEM)
    dma = pltpu.SemaphoreType.DMA
    scratch = [
        pltpu.VMEM((rows, width), BF16),
        pltpu.VMEM((NX, NZ, NC, OWN, width), BF16),
        pltpu.VMEM((width, width), BF16),
        pltpu.VMEM((8, 128), F32),
        pltpu.VMEM((8, 128), jnp.int32),
        pltpu.VMEM((8, 128), jnp.int32),
        pltpu.VMEM((rows, rows), F32),
        pltpu.VMEM((rows, rows), BF16),
        pltpu.VMEM((rows, 128), F32),
        pltpu.VMEM((rows, 128), F32),
        pltpu.VMEM((8, 128), F32),
        pltpu.VMEM((NY - 1, 8, 128), F32),
        pltpu.VMEM((NY, span + 16, 128), BF16),
        pltpu.VMEM((NY - 1, span + 16, 128), BF16),
        pltpu.VMEM((span, rows), F32),
    ]
    scratch += [pltpu.VMEM((half, w), kind) for kind in (F32, BF16, BF16) for w in (width, 128)]
    widths = [b - a for a, b in zip(EDGES, EDGES[1:])]
    scratch += [pltpu.VMEM((6, 64, w), BF16) for w in widths] * 2
    turns = [pltpu.VMEM((NZ - 1, OWN, w), BF16) for w in widths]
    turns += [pltpu.VMEM((NZ - 1, NX, OWN, 128), BF16)]
    scratch += turns * 2 + [pltpu.VMEM((NX, OWN, 128), F32), pltpu.VMEM((NX - 1, OWN, 128), F32)]
    scratch += [pltpu.VMEM((NX, OWN, 128), F32)]
    scratch += [dma((9,)), dma((14,)), dma((17,))]
    updated, moments = pl.pallas_call(
        kernel,
        out_shape=(
            jax.ShapeDtypeStruct((OWN, width), F32),
            jax.ShapeDtypeStruct((OWN, span), F32),
        ),
        in_specs=[any_spec] * 6,
        out_specs=(vmem_spec, vmem_spec),
        scratch_shapes=scratch,
        compiler_params=pltpu.CompilerParams(
            collective_id=0, has_side_effects=True, vmem_limit_bytes=40000 * 1024
        ),
    )(*(pltpu.with_memory_space_constraint(a, pltpu.HBM) for a in (
        vectors,
        centroids.reshape(NX, NZ, NC, OWN, width),
        rotation,
        prior_mass.reshape(8, 128),
        assign.reshape(8, 128),
        owner_of.reshape(NY, 8, 128),
    )))
    return (updated[None], moments[None])


def solution(mesh):
    finer = Mesh(
        mesh.devices.reshape(NX, NZ, NC, mesh.shape["cent"]), ("dp_0", "dp_1", "dp_2", "cent")
    )
    in_specs = (P(DP, None), P("cent", None), P("cent"), P(DP), P(), P())
    out_specs = (P("cent", DP, None), P(DP, None, "cent"))
    return jax.shard_map(body, mesh=finer, in_specs=in_specs, out_specs=out_specs, check_vma=False)
```
